32 devices in a mesh: groups: 2 (over y), blk: 16 (over z, x, core).
Axes of the slice: x: 2, y: 2, z: 4, core: 2. Of those that a mesh axis runs over, the one named last changes fastest.
Arguments:
- queries: bfloat16 [2048, 2048], P(('groups', 'blk')), parts along dimension 0, may hold values from -48 to 48
- rotated_cache_keys: bfloat16 [16384, 256], P(('groups', 'blk')), parts along dimension 0, may hold values from -4 to 4
- stored_cache_values: bfloat16 [16384, 256], P(('groups', 'blk')), parts along dimension 0, may hold values from -5 to 5
- segment_new_keys: bfloat16 [2048, 256], P(('groups', 'blk')), parts along dimension 0, may hold values from -4 to 4
- segment_new_values: bfloat16 [2048, 256], P(('groups', 'blk')), parts along dimension 0, may hold values from -5 to 5
- block_ids: int32 [2048, 8], P(('groups', 'blk')), parts along dimension 0, may hold values from 0 to 15, all different within a row; in each aligned block of 64 rows (0 to 63, 64 to 127, ...) at most 40 rows name the same one
- residual_in: bfloat16 [2048, 1024], P(('groups', 'blk')), parts along dimension 0, may hold values from -3 to 3
- out_weight: bfloat16 [2048, 1024], replicated, may hold values from -1.5 to 1.5
- norm_gain: float32 [1024], replicated, may hold values from 0.25 to 1.75
- expert_ids: int32 [2048, 8], P(('groups', 'blk')), parts along dimension 0, may hold values from 0 to 15, all different within a row; in each aligned block of 64 rows (0 to 63, 64 to 127, ...) at most 48 rows name the same one
- gate_scores: float32 [2048, 8], P(('groups', 'blk')), parts along dimension 0, may hold values from 0.05 to 1
- w_gate: bfloat16 [16, 1024, 768], P('blk'), may hold values from -0.1875 to 0.1875
- w_up: bfloat16 [16, 1024, 768], P('blk'), may hold values from -0.1875 to 0.1875
- w_down: bfloat16 [16, 768, 1024], P('blk'), may hold values from -0.21875 to 0.21875
Outputs:
- layer_out: bfloat16 [2048, 1024], P(('groups', 'blk')), parts along dimension 0
The draws below stay inside these ranges and needn't reach their ends.
There are 2 independent parts, one for each index of `groups`. The reference program is written for one: setup_inputs(seed, part) draws one part's arguments, and reference() takes and returns one part's arrays. A program takes and returns all parts, laid end to end along the dimension named above; an argument that names none is the same for every part. Nothing has to cross between parts.
Inputs may be any that keep to these rules, and one draw needn't show every extreme that they name: `block_ids`: each row names 8 different blocks. Among the rows of one device no block is named more than 40 times, and in some devices' rows some block is named exactly 40 times. `expert_ids`: each row names 8 different experts. Among the rows of one device no expert is named more than 48 times, and in some devices' rows some expert is named exactly 48 times.
All inputs are finite; a program needn't handle non-finite values.
Results may differ from the reference program's by a relative error of at most 0.0095.
Values may be sent and summed in bfloat16 or wider, within the bound.
A program may use at most 128 MiB of HBM per device.

```python
import math
import jax
import jax.numpy as jnp
import numpy as np
from jax import lax

D = 1024
QUERY_HEADS = 16
KEY_VALUE_HEADS = 2
HEAD_SIZE = 128
FF = 768
TOPB = 8
TOPE = 8
TOKENS_PER_SHARD = 64
BLOCK_TOKENS = 512
SEGMENT_TOKENS = 1024
EXPERTS = 16
CAP = 40
CAP_E = 48
N_BLK = 16


def paired_draw(key):
    base = jax.random.fold_in(key, 11)
    first, latter_portion = jax.random.split(base, 2)
    query_vals = jnp.clip(jax.random.normal(first, (SEGMENT_TOKENS, QUERY_HEADS * HEAD_SIZE), jnp.float32), -4.0, 4.0)
    key_value_pairs = jnp.clip(jax.random.normal(latter_portion, (SEGMENT_TOKENS, KEY_VALUE_HEADS * HEAD_SIZE), jnp.float32), -4.0, 4.0)
    return (query_vals, key_value_pairs)


def draw_queries(key, part):
    return paired_draw(key)[0].astype(jnp.bfloat16)


def draw_segment_new_keys(key, part):
    return paired_draw(key)[1].astype(jnp.bfloat16)


def steps_of(own_key, extent, shards, low, largest):
    def one(axis_at, blocks):
        steps = jax.random.uniform(jax.random.fold_in(jax.random.fold_in(own_key, 6), axis_at), (blocks,), jnp.float32, low / len(shards), largest / len(shards))
        return jnp.repeat(jnp.exp(steps), extent[axis_at] // blocks).reshape((-1,) + (1,) * (len(extent) - axis_at - 1))

    loudness = one(*shards[0])
    for cut in shards[1:]:
        loudness = loudness * one(*cut)
    return loudness


def assign_block(rng, own, number, rows, number_of, top, reach, lean):
    sequence = jax.random.permutation(rng, number_of)
    packed, usual = portions_of(number_of, rows * top, reach, lean, True), portions_of(number_of, rows * top, reach, lean, False)
    places = jnp.arange(number_of)

    def named(lengths, rotation):
        used = int((lengths > 0).sum())
        fixed = max(1, used // 4)
        moved = fixed + (places - fixed + rotation * (used - fixed)) % max(1, number_of - fixed)
        return jnp.zeros((number_of,), jnp.int32).at[sequence[jnp.where(places < fixed, places, moved)]].set(jnp.asarray(lengths, jnp.int32))

    lengths = jnp.where(number % 4 == 0, named(packed, number // 4), named(usual, number - number // 4 - 1))
    mixed = jax.random.permutation(jax.random.fold_in(own, 3), number_of)
    donor, taker = mixed[0:number_of // 2 * 2:2], mixed[1:number_of // 2 * 2:2]
    room = jnp.minimum(lengths[donor] - 1, reach - lengths[taker]) // 2
    room = jnp.where((donor == sequence[0]) | (taker == sequence[0]) | (lengths[taker] == 0), 0, jnp.maximum(room, 0))
    moved = jax.random.randint(jax.random.fold_in(own, 4), (number_of // 2,), 0, 1 << 20) % (room + 1)
    lengths = lengths.at[donor].add(-moved).at[taker].add(moved)
    items = jnp.searchsorted(jnp.cumsum(lengths), jnp.arange(rows * top), side="right").astype(jnp.int32)
    listing = items.reshape(top, rows).T
    listing = listing[jax.random.permutation(jax.random.fold_in(own, 1), rows)]
    rotation = jax.random.randint(jax.random.fold_in(own, 2), (rows, 1), 0, top)
    return jnp.take_along_axis(listing, (jnp.arange(top)[None, :] + rotation) % top, axis=1)


def portions_of(number_of, total, bound, lean, full):
    weights = [(1 << 20) // math.isqrt(standing ** lean) + 1 for standing in range(1, number_of + 1)]
    largest = bound if full else min(bound, max(-(-total // number_of), total * weights[0] // sum(weights)))
    least = 1 if total - largest >= number_of - 1 else 0
    counts, surplus = [largest] + [least] * (number_of - 1), total - largest - least * (number_of - 1)
    while surplus > 0:
        candidates = [i for i in range(1, number_of) if counts[i] < largest] or [i for i in range(1, number_of) if counts[i] < bound]
        whole, budget = sum([weights[i] for i in candidates]), surplus
        for i in candidates:
            extra = min(bound - counts[i], max(1, budget * weights[i] // whole), surplus)
            counts[i] = counts[i] + extra
            surplus = surplus - extra
    return np.array(counts)


def bell_draw(rng, dims, spread, most, pieces=(), held_as=jnp.bfloat16):
    factor_of = steps_of(rng, dims, pieces, -0.22, 0.18) if pieces else 1.0
    values = jax.random.normal(rng, dims, jnp.float32) * spread * factor_of
    return jnp.minimum(jnp.maximum(values, -most), most).astype(held_as)


def setup_inputs(seed: int = 0, part: int = 0) -> dict:
    splits = jax.random.split(jax.random.key(seed), 15)
    own_keys = jax.random.split(jax.random.fold_in(splits[14], part), 15)
    queries = draw_queries(jax.random.fold_in(jax.random.fold_in(splits[14], part), 71), part)
    rotated_cache_keys = bell_draw(own_keys[1], (N_BLK * BLOCK_TOKENS, KEY_VALUE_HEADS * HEAD_SIZE), 1.0, 4.0, ((0, 16),))
    stored_cache_values = bell_draw(own_keys[2], (N_BLK * BLOCK_TOKENS, KEY_VALUE_HEADS * HEAD_SIZE), 1.0, 5.0, ((0, 16),))
    segment_new_keys = draw_segment_new_keys(jax.random.fold_in(jax.random.fold_in(splits[14], part), 71), part)
    segment_new_values = bell_draw(own_keys[4], (SEGMENT_TOKENS, KEY_VALUE_HEADS * HEAD_SIZE), 1.0, 5.0, ((0, 16),))
    block_ids_keys = jax.random.split(jax.random.fold_in(own_keys[5], 1), SEGMENT_TOKENS // TOKENS_PER_SHARD)
    block_ids_turns = jax.random.permutation(jax.random.fold_in(own_keys[5], 3), SEGMENT_TOKENS // TOKENS_PER_SHARD)
    block_ids = jax.vmap(lambda own, number: assign_block(jax.random.fold_in(own_keys[5], 2), own, number, TOKENS_PER_SHARD, N_BLK, TOPB, CAP, 2))(block_ids_keys, block_ids_turns).reshape((SEGMENT_TOKENS, TOPB))
    residual_in = bell_draw(own_keys[6], (SEGMENT_TOKENS, D), 0.5, 3.0, ((0, 16),))
    out_weight = bell_draw(splits[7], (QUERY_HEADS * HEAD_SIZE, D), 16 ** -0.5, 1.5)
    norm_gain = jnp.clip(1.0 + 0.15 * jax.random.normal(splits[8], (D,), jnp.float32), 0.25, 1.75)
    expert_ids_keys = jax.random.split(jax.random.fold_in(own_keys[9], 1), SEGMENT_TOKENS // TOKENS_PER_SHARD)
    expert_ids_turns = jax.random.permutation(jax.random.fold_in(own_keys[9], 3), SEGMENT_TOKENS // TOKENS_PER_SHARD)
    expert_ids = jax.vmap(lambda own, number: assign_block(jax.random.fold_in(own_keys[9], 2), own, number, TOKENS_PER_SHARD, EXPERTS, TOPE, CAP_E, 2))(expert_ids_keys, expert_ids_turns).reshape((SEGMENT_TOKENS, TOPE))
    gate_scores = jnp.clip(jnp.exp(math.log(1.0) - 2.9957323 * jax.random.uniform(own_keys[10], (SEGMENT_TOKENS, TOPE), jnp.float32) ** steps_of(own_keys[10], (SEGMENT_TOKENS, TOPE), ((0, 16),), -0.2, 0.2)), 0.05, 1.0)
    w_gate = bell_draw(splits[11], (EXPERTS, D, FF), D ** -0.5, 0.1875, ((0, 16),))
    w_up = bell_draw(splits[12], (EXPERTS, D, FF), D ** -0.5, 0.1875, ((0, 16),))
    w_down = bell_draw(splits[13], (EXPERTS, FF, D), FF ** -0.5, 0.21875, ((0, 16),))
    return {"queries": queries, "rotated_cache_keys": rotated_cache_keys, "stored_cache_values": stored_cache_values, "segment_new_keys": segment_new_keys, "segment_new_values": segment_new_values, "block_ids": block_ids, "residual_in": residual_in, "out_weight": out_weight, "norm_gain": norm_gain, "expert_ids": expert_ids, "gate_scores": gate_scores, "w_gate": w_gate, "w_up": w_up, "w_down": w_down}


NORM_EPSILON = 1e-06

def settle(values):
    return lax.optimization_barrier(values.astype(jnp.bfloat16)).astype(jnp.float32)

def reference(queries, rotated_cache_keys, stored_cache_values, segment_new_keys, segment_new_values, block_ids, residual_in, out_weight, norm_gain, expert_ids, gate_scores, w_gate, w_up, w_down):
    queries_per_cluster = QUERY_HEADS // KEY_VALUE_HEADS
    score_scale = HEAD_SIZE ** (-0.5)
    blocked_keys = rotated_cache_keys.reshape(N_BLK, BLOCK_TOKENS, KEY_VALUE_HEADS, HEAD_SIZE)
    blocked_values = stored_cache_values.reshape(N_BLK, BLOCK_TOKENS, KEY_VALUE_HEADS, HEAD_SIZE)

    def local_segment(inputs):
        segment_queries, segment_keys, segment_values = inputs
        heads_of_queries = segment_queries.astype(jnp.float32).reshape(TOKENS_PER_SHARD, KEY_VALUE_HEADS, queries_per_cluster, HEAD_SIZE)
        heads_of_keys = segment_keys.astype(jnp.float32).reshape(TOKENS_PER_SHARD, KEY_VALUE_HEADS, HEAD_SIZE)
        heads_of_values = segment_values.astype(jnp.float32).reshape(TOKENS_PER_SHARD, KEY_VALUE_HEADS, HEAD_SIZE)
        scores = jnp.einsum('qhgd,khd->qhgk', heads_of_queries, heads_of_keys) * score_scale
        places = jnp.arange(TOKENS_PER_SHARD, dtype=jnp.int32)
        allowed = places[None, :] <= places[:, None]
        scores = jnp.where(allowed[:, None, None, :], scores, -jnp.inf)
        row_max = lax.optimization_barrier(jnp.max(scores, axis=-1))
        weights = jnp.exp(scores - row_max[..., None])
        row_total = lax.optimization_barrier(jnp.sum(weights, axis=-1))
        merged = jnp.einsum('qhgk,khd->qhgd', settle(weights), heads_of_values)
        return (row_max.reshape(TOKENS_PER_SHARD, QUERY_HEADS), row_total.reshape(TOKENS_PER_SHARD, QUERY_HEADS), merged.reshape(TOKENS_PER_SHARD, QUERY_HEADS, HEAD_SIZE))
    local_row_maximum, local_denominator, local_output = lax.map(local_segment, (queries.reshape(N_BLK, TOKENS_PER_SHARD, QUERY_HEADS * HEAD_SIZE), segment_new_keys.reshape(N_BLK, TOKENS_PER_SHARD, KEY_VALUE_HEADS * HEAD_SIZE), segment_new_values.reshape(N_BLK, TOKENS_PER_SHARD, KEY_VALUE_HEADS * HEAD_SIZE)))
    local_row_maximum = local_row_maximum.reshape(SEGMENT_TOKENS // 16, 16, QUERY_HEADS)
    local_denominator = local_denominator.reshape(SEGMENT_TOKENS // 16, 16, QUERY_HEADS)
    local_output = local_output.reshape(SEGMENT_TOKENS // 16, 16, QUERY_HEADS, HEAD_SIZE)

    def cache_part(inputs):
        shard_queries, part_ids, part_max, part_total, part_out = inputs
        heads_of_queries = shard_queries.astype(jnp.float32).reshape(16, KEY_VALUE_HEADS, queries_per_cluster, HEAD_SIZE)
        chosen_keys = blocked_keys[part_ids].astype(jnp.float32)
        chosen_values = blocked_values[part_ids].astype(jnp.float32)
        scores = jnp.einsum('rhgd,rjkhd->rjhgk', heads_of_queries, chosen_keys) * score_scale
        row_max = lax.optimization_barrier(jnp.max(scores, axis=-1))
        weights = jnp.exp(scores - row_max[..., None])
        row_total = lax.optimization_barrier(jnp.sum(weights, axis=-1))
        merged = settle(jnp.einsum('rjhgk,rjkhd->rjhgd', settle(weights), chosen_values))
        row_max = row_max.reshape(16, TOPB, QUERY_HEADS)
        row_total = row_total.reshape(16, TOPB, QUERY_HEADS)
        merged = merged.reshape(16, TOPB, QUERY_HEADS, HEAD_SIZE)
        ceiling = jnp.maximum(part_max, lax.optimization_barrier(jnp.max(row_max, axis=1)))
        own_scale = jnp.exp(part_max - ceiling)
        pair_scale = jnp.exp(row_max - ceiling[:, None, :])
        denominator = part_total * own_scale + lax.optimization_barrier(jnp.sum(row_total * pair_scale, axis=1))
        numerator = part_out * own_scale[:, :, None] + lax.optimization_barrier(jnp.sum(merged * pair_scale[:, :, :, None], axis=1))
        return (numerator / denominator[:, :, None]).reshape(16, QUERY_HEADS * HEAD_SIZE).astype(jnp.bfloat16)
    attention = lax.map(cache_part, (queries.reshape(SEGMENT_TOKENS // 16, 16, QUERY_HEADS * HEAD_SIZE), block_ids.astype(jnp.int32).reshape(SEGMENT_TOKENS // 16, 16, TOPB), local_row_maximum, local_denominator, local_output))
    attention = attention.reshape(SEGMENT_TOKENS, QUERY_HEADS * HEAD_SIZE)
    hidden_state = residual_in.astype(jnp.float32) + jnp.dot(attention, out_weight, preferred_element_type=jnp.float32)
    normed = (hidden_state * lax.rsqrt(lax.optimization_barrier(jnp.mean(hidden_state * hidden_state, axis=-1, keepdims=True)) + NORM_EPSILON) * norm_gain.astype(jnp.float32)).astype(jnp.bfloat16)
    flat_experts = expert_ids.reshape(-1).astype(jnp.int32)
    pair_total = SEGMENT_TOKENS * TOPE
    ordering = jnp.argsort(flat_experts, stable=True).astype(jnp.int32)
    loads = lax.optimization_barrier(jnp.sum((flat_experts[:, None] == jnp.arange(EXPERTS, dtype=jnp.int32)[None, :]).astype(jnp.int32), axis=0))
    starts = jnp.cumsum(loads) - loads
    mixing = (gate_scores / lax.optimization_barrier(jnp.sum(gate_scores, axis=1, keepdims=True))).reshape(-1)

    def one_expert(accum, inputs):
        gate_matrix, up_matrix, down_matrix, start_at, load_of = inputs
        places = jnp.arange(N_BLK * CAP_E, dtype=jnp.int32)
        picked = ordering[jnp.minimum(start_at + places, pair_total - 1)]
        token_of = (picked // TOPE).astype(jnp.int32)
        rows_in = normed[token_of]
        gate_part = jnp.dot(rows_in, gate_matrix, preferred_element_type=jnp.float32)
        up_part = jnp.dot(rows_in, up_matrix, preferred_element_type=jnp.float32)
        inner = (jax.nn.silu(gate_part) * up_part).astype(jnp.bfloat16)
        expert_out = settle(jnp.dot(inner, down_matrix, preferred_element_type=jnp.float32))
        weight_of = jnp.where(places < load_of, mixing[picked], jnp.zeros((), mixing.dtype))
        accum = accum.at[token_of].add(weight_of[:, None] * expert_out)
        return (accum, None)
    mixture, unused = lax.scan(one_expert, jnp.zeros((SEGMENT_TOKENS, D), jnp.float32), (w_gate, w_up, w_down, starts.astype(jnp.int32), loads.astype(jnp.int32)))
    return (hidden_state + mixture).astype(jnp.bfloat16)
```

```python
import functools

import jax
import jax.numpy as jnp
from jax import lax
from jax.experimental import pallas as pl
from jax.experimental.pallas import tpu as pltpu
from jax.sharding import PartitionSpec as P

QUERY_HEADS = 16
KEY_VALUE_HEADS = 2
HEAD_SIZE = 128
TOPB = 8
TOPE = 8


NORM_EPSILON = 1e-06


def partials(query_rows, key_rows, value_rows, causal):
    queries_per_cluster = QUERY_HEADS // KEY_VALUE_HEADS
    score_scale = HEAD_SIZE ** (-0.5)
    maxima = []
    totals = []
    outputs = []
    for head_cluster in range(KEY_VALUE_HEADS):
        offset = head_cluster * queries_per_cluster * HEAD_SIZE
        group_queries = query_rows[:, offset : offset + queries_per_cluster * HEAD_SIZE].reshape(
            -1, HEAD_SIZE
        )
        group_keys = key_rows[:, head_cluster * HEAD_SIZE : (head_cluster + 1) * HEAD_SIZE]
        group_values = value_rows[:, head_cluster * HEAD_SIZE : (head_cluster + 1) * HEAD_SIZE]
        scores = (
            lax.dot_general(
                group_queries,
                group_keys,
                (((1,), (1,)), ((), ())),
                preferred_element_type=jnp.float32,
            )
            * score_scale
        )
        if causal:
            owner_row = jnp.arange(group_queries.shape[0], dtype=jnp.int32) // queries_per_cluster
            key_place = jnp.arange(key_rows.shape[0], dtype=jnp.int32)
            scores = jnp.where(key_place[None, :] <= owner_row[:, None], scores, -jnp.inf)
        row_max = jnp.max(scores, axis=1)
        weights = jnp.exp(scores - row_max[:, None])
        maxima.append(row_max.reshape(-1, queries_per_cluster))
        totals.append(jnp.sum(weights, axis=1).reshape(-1, queries_per_cluster))
        mixed_rows = jnp.dot(
            weights.astype(jnp.bfloat16), group_values, preferred_element_type=jnp.float32
        )
        outputs.append(mixed_rows.reshape(-1, queries_per_cluster * HEAD_SIZE))
    return (
        jnp.concatenate(maxima, axis=1),
        jnp.concatenate(totals, axis=1),
        jnp.concatenate(outputs, axis=1),
    )


def bucket_slots(targets, capacity, parties):
    flat_targets = targets.reshape(-1)
    pair_count = flat_targets.shape[0]
    one_hot = (flat_targets[:, None] == jnp.arange(parties, dtype=jnp.int32)[None, :]).astype(
        jnp.int32
    )
    before = jnp.sum((jnp.cumsum(one_hot, axis=0) - one_hot) * one_hot, axis=1)
    slot_index = flat_targets * capacity + before
    filler = (
        jnp.full((parties * capacity,), pair_count, jnp.int32)
        .at[slot_index]
        .set(jnp.arange(pair_count, dtype=jnp.int32))
    )
    return (slot_index, filler)


def body(
    queries,
    rotated_cache_keys,
    stored_cache_values,
    segment_new_keys,
    segment_new_values,
    block_ids,
    residual_in,
    out_weight,
    norm_gain,
    expert_ids,
    gate_scores,
    w_gate,
    w_up,
    w_down,
):
    parties = lax.axis_size("blk")
    tok_count = queries.shape[0]
    capacity = tok_count * TOPB * 5 // (4 * parties)
    expert_capacity = tok_count * TOPE * 3 // (2 * parties)
    owner_slots, slot_pair = bucket_slots(block_ids, capacity, parties)
    pair_count = tok_count * TOPB
    occupied = slot_pair < pair_count
    source_token = jnp.minimum(slot_pair, pair_count - 1) // TOPB
    outgoing = jnp.where(
        occupied[:, None], queries[source_token], jnp.zeros((), queries.dtype)
    ).reshape(parties, capacity, QUERY_HEADS * HEAD_SIZE)
    arrived = lax.all_to_all(outgoing, "blk", split_axis=0, concat_axis=0, tiled=True)
    senders, items, row_width = arrived.shape
    far_max, far_total, far_out = partials(
        arrived.reshape(senders * items, row_width), rotated_cache_keys, stored_cache_values, False
    )
    back_max = lax.all_to_all(
        far_max.reshape(senders, items, QUERY_HEADS), "blk", split_axis=0, concat_axis=0, tiled=True
    )
    back_total = lax.all_to_all(
        far_total.reshape(senders, items, QUERY_HEADS),
        "blk",
        split_axis=0,
        concat_axis=0,
        tiled=True,
    )
    back_out = lax.all_to_all(
        far_out.astype(jnp.bfloat16).reshape(senders, items, row_width),
        "blk",
        split_axis=0,
        concat_axis=0,
        tiled=True,
    )
    local_row_maximum, local_denominator, local_output = partials(
        queries, segment_new_keys, segment_new_values, True
    )
    pair_max = back_max.reshape(-1, QUERY_HEADS)[owner_slots].reshape(tok_count, TOPB, QUERY_HEADS)
    pair_total = back_total.reshape(-1, QUERY_HEADS)[owner_slots].reshape(
        tok_count, TOPB, QUERY_HEADS
    )
    pair_out = back_out.reshape(-1, QUERY_HEADS * HEAD_SIZE)[owner_slots].reshape(
        tok_count, TOPB, QUERY_HEADS, HEAD_SIZE
    )
    ceiling = jnp.maximum(local_row_maximum, jnp.max(pair_max, axis=1))
    own_scale = jnp.exp(local_row_maximum - ceiling)
    pair_scale = jnp.exp(pair_max - ceiling[:, None, :])
    denominator = local_denominator * own_scale + jnp.sum(pair_total * pair_scale, axis=1)
    numerator = local_output.reshape(tok_count, QUERY_HEADS, HEAD_SIZE) * own_scale[
        :, :, None
    ] + jnp.einsum("tjh,tjhd->thd", pair_scale, pair_out, preferred_element_type=jnp.float32)
    attention = (
        (numerator / denominator[:, :, None])
        .reshape(tok_count, QUERY_HEADS * HEAD_SIZE)
        .astype(jnp.bfloat16)
    )
    hidden_state = residual_in.astype(jnp.float32) + jnp.dot(
        attention, out_weight, preferred_element_type=jnp.float32
    )
    normed = (
        hidden_state
        * lax.rsqrt(jnp.mean(hidden_state * hidden_state, axis=-1, keepdims=True) + NORM_EPSILON)
        * norm_gain
    ).astype(jnp.bfloat16)
    expert_slots, expert_pair = bucket_slots(expert_ids, expert_capacity, parties)
    expert_pairs = tok_count * TOPE
    expert_used = expert_pair < expert_pairs
    expert_token = jnp.minimum(expert_pair, expert_pairs - 1) // TOPE
    dispatched = jnp.where(
        expert_used[:, None], normed[expert_token], jnp.zeros((), normed.dtype)
    ).reshape(parties, expert_capacity, normed.shape[1])
    arrived = lax.all_to_all(dispatched, "blk", split_axis=0, concat_axis=0, tiled=True)
    flat_rows = arrived.reshape(-1, arrived.shape[2])
    gate_part = jnp.dot(flat_rows, w_gate[0], preferred_element_type=jnp.float32)
    up_part = jnp.dot(flat_rows, w_up[0], preferred_element_type=jnp.float32)
    inner = (jax.nn.silu(gate_part) * up_part).astype(jnp.bfloat16)
    expert_out = (
        jnp.dot(inner, w_down[0], preferred_element_type=jnp.float32)
        .astype(jnp.bfloat16)
        .reshape(arrived.shape)
    )
    returned = lax.all_to_all(expert_out, "blk", split_axis=0, concat_axis=0, tiled=True)
    gathered_rows = returned.reshape(-1, normed.shape[1])[expert_slots].reshape(
        tok_count, TOPE, normed.shape[1]
    )
    mixing = gate_scores / jnp.sum(gate_scores, axis=1, keepdims=True)
    mixture = jnp.einsum("tk,tkd->td", mixing, gathered_rows, preferred_element_type=jnp.float32)
    return (hidden_state + mixture).astype(jnp.bfloat16)


LANES = 128
LOW_PART = 64
MESH = pl.DeviceIdType.MESH
LOG2_E = 1.4426950408889634


def place_of(index):
    return lax.div(index, 4), lax.rem(lax.div(index, 2), 2), lax.rem(index, 2)


def index_of(z, x, c):
    return (z * 2 + x) * 2 + c


def nth_plane(k, z, planes):
    low = jnp.minimum(z, planes - 1 - z)
    near = k <= 2 * low
    far = jnp.where(near, lax.div(k + 1, 2), k - low)
    up = jnp.where(near, lax.rem(k, 2), (z < planes - 1 - z).astype(jnp.int32))
    return z + far * (2 * up - 1)


class Gather:
    def __init__(self, planes, bufs, send_sem, recv_sem):
        self.planes, self.bufs, self.send_sem, self.recv_sem = planes, bufs, send_sem, recv_sem
        self.me = lax.axis_index("blk")
        self.z, self.x, self.c = place_of(self.me)

    def copy(self, part, way, block, target):
        return pltpu.make_async_remote_copy(
            src_ref=self.bufs[part].at[block],
            dst_ref=self.bufs[part].at[block],
            send_sem=self.send_sem.at[part, way, block],
            recv_sem=self.recv_sem.at[part, block],
            device_id={"blk": target},
            device_id_type=MESH,
        )

    def arrive(self, part, block):
        self.copy(part, 3, block, index_of(self.z, self.x, 1 - self.c)).wait_recv()

    def column_ways(self, plane):
        up = jnp.logical_and(plane <= self.z, self.z < self.planes - 1)
        down = jnp.logical_and(plane >= self.z, self.z > 0)
        return up, down

    def pass_column(self, part, plane):
        z, x, c = self.z, self.x, self.c
        block = index_of(plane, x, c)
        up, down = self.column_ways(plane)

        @pl.when(up)
        def _():
            self.copy(part, 0, block, index_of(z + 1, x, c)).start()

        @pl.when(down)
        def _():
            self.copy(part, 1, block, index_of(z - 1, x, c)).start()

        self.copy(part, 2, block, index_of(z, 1 - x, c)).start()
        self.copy(part, 3, block, index_of(z, x, 1 - c)).start()

    def take_column(self, k):
        plane = nth_plane(k, self.z, self.planes)
        for part in range(len(self.bufs)):

            @pl.when(k > 0)
            def _():
                self.arrive(part, index_of(plane, self.x, self.c))

            self.pass_column(part, plane)

    def take_across(self, k):
        plane = nth_plane(k, self.z, self.planes)
        block = index_of(plane, 1 - self.x, self.c)
        for part in range(len(self.bufs)):
            self.arrive(part, block)
            self.copy(part, 3, block, index_of(self.z, self.x, 1 - self.c)).start()

    def take_partner(self, k, x):
        plane = nth_plane(k, self.z, self.planes)
        for part in range(len(self.bufs)):
            self.arrive(part, index_of(plane, x, 1 - self.c))

    def finish(self):
        z, x, c = self.z, self.x, self.c

        @pl.loop(0, self.planes)
        def _(plane):
            block = index_of(plane, x, c)
            across = index_of(plane, 1 - x, c)
            up, down = self.column_ways(plane)
            for part in range(len(self.bufs)):

                @pl.when(up)
                def _():
                    self.copy(part, 0, block, index_of(z + 1, x, c)).wait_send()

                @pl.when(down)
                def _():
                    self.copy(part, 1, block, index_of(z - 1, x, c)).wait_send()

                self.copy(part, 2, block, index_of(z, 1 - x, c)).wait_send()
                self.copy(part, 3, block, index_of(z, x, 1 - c)).wait_send()
                self.copy(part, 3, across, index_of(z, x, 1 - c)).wait_send()


def greet(planes, z, x, c):
    barrier = pltpu.get_barrier_semaphore()
    for target in (index_of(z, 1 - x, c), index_of(z, x, 1 - c)):
        pl.semaphore_signal(barrier, inc=1, device_id={"blk": target}, device_id_type=MESH)

    @pl.loop(0, planes)
    def _(plane):
        @pl.when(plane != z)
        def _():
            pl.semaphore_signal(
                barrier, inc=1, device_id={"blk": index_of(plane, x, c)}, device_id_type=MESH
            )

    pl.semaphore_wait(barrier, planes + 1)


def attention_kernel(
    planes,
    q_ref,
    k_any,
    v_any,
    new_k_ref,
    new_v_ref,
    ids_ref,
    residual_ref,
    weight_any,
    gain_ref,
    experts_ref,
    gates_ref,
    hidden_ref,
    rows_ref,
    k_buf,
    v_buf,
    weight_buf,
    q_buf,
    att_buf,
    max_buf,
    sum_buf,
    acc_buf,
    local_sem,
    send_sem,
    recv_sem,
):
    gather = Gather(planes, (k_buf, v_buf), send_sem, recv_sem)
    me, z, x, c = gather.me, gather.z, gather.x, gather.c
    own = [
        pltpu.make_async_copy(k_any, k_buf.at[me], local_sem.at[0]),
        pltpu.make_async_copy(v_any, v_buf.at[me], local_sem.at[1]),
    ]
    weights_in = pltpu.make_async_copy(weight_any, weight_buf, local_sem.at[2])
    for copy in own:
        copy.start()
    greet(planes, z, x, c)
    for copy in own:
        copy.wait()
    gather.take_column(jnp.int32(0))
    weights_in.start()

    tokens = q_ref.shape[0]
    chunks, chunk_rows, _ = q_buf.shape
    heads = chunk_rows // tokens
    chunks_per_group = chunks // KEY_VALUE_HEADS
    factor = HEAD_SIZE ** (-0.5) * LOG2_E

    for chunk in range(chunks):
        group = chunk // chunks_per_group
        lanes = slice(group * HEAD_SIZE, (group + 1) * HEAD_SIZE)
        for head in range(heads):
            at = (chunk * heads + head) * HEAD_SIZE
            q_buf[chunk, head * tokens : (head + 1) * tokens, :] = q_ref[:, at : at + HEAD_SIZE]
        scores = lax.dot_general(
            q_buf[chunk],
            new_k_ref[:, lanes],
            (((1,), (1,)), ((), ())),
            preferred_element_type=jnp.float32,
        )
        row = lax.rem(lax.broadcasted_iota(jnp.int32, scores.shape, 0), tokens)
        key = lax.broadcasted_iota(jnp.int32, scores.shape, 1)
        scores = jnp.where(key <= row, scores, -jnp.inf)
        top = jnp.max(scores, axis=1, keepdims=True)
        weights = jnp.exp2((scores - top) * factor)
        max_buf[chunk] = top
        sum_buf[chunk] = jnp.sum(weights, axis=1, keepdims=True)
        acc_buf[chunk] = jnp.dot(
            weights.astype(jnp.bfloat16), new_v_ref[:, lanes], preferred_element_type=jnp.float32
        )

    @pl.loop(0, 4 * (planes + 1))
    def _(step):
        k, kind = lax.div(step, 4), lax.rem(step, 4)
        late = lax.div(kind, 2)
        valid = jnp.logical_or(
            jnp.logical_and(late == 0, k < planes), jnp.logical_and(late == 1, k > 0)
        )

        @pl.when(valid)
        def _():
            place = k - late
            plane = nth_plane(place, z, planes)

            @pl.when(jnp.logical_and(kind == 0, k > 0))
            def _():
                gather.take_column(k)

            @pl.when(kind == 1)
            def _():
                gather.take_partner(place, x)

            @pl.when(kind == 2)
            def _():
                gather.take_across(place)

            @pl.when(kind == 3)
            def _():
                gather.take_partner(place, 1 - x)

            other_core = lax.rem(kind, 2)
            block = index_of(
                plane,
                x + late * (1 - 2 * x),
                c + other_core * (1 - 2 * c),
            )
            named = jnp.sum(
                jnp.where(ids_ref[...] == block, jnp.float32(1), jnp.float32(0)),
                axis=1,
                keepdims=True,
            )
            named = jnp.concatenate([named] * heads, axis=0) > 0.5
            for chunk in range(chunks):
                group = chunk // chunks_per_group
                lanes = slice(group * HEAD_SIZE, (group + 1) * HEAD_SIZE)
                scores = lax.dot_general(
                    q_buf[chunk],
                    k_buf[block, :, lanes],
                    (((1,), (1,)), ((), ())),
                    preferred_element_type=jnp.float32,
                )
                before = max_buf[chunk]
                top = jnp.maximum(before, jnp.max(scores, axis=1, keepdims=True))
                weights = jnp.exp2((scores - top) * factor)
                scale = jnp.where(named, jnp.exp2((before - top) * factor), 1.0)
                total = jnp.sum(weights, axis=1, keepdims=True)
                mixed = jnp.dot(
                    weights.astype(jnp.bfloat16),
                    v_buf[block, :, lanes],
                    preferred_element_type=jnp.float32,
                )
                max_buf[chunk] = jnp.where(named, top, before)
                sum_buf[chunk] = sum_buf[chunk] * scale + jnp.where(named, total, 0.0)
                acc_buf[chunk] = acc_buf[chunk] * scale + jnp.where(named, mixed, 0.0)

    for chunk in range(chunks):
        attention = (acc_buf[chunk] / sum_buf[chunk]).astype(jnp.bfloat16)
        for head in range(heads):
            at = (chunk * heads + head) * HEAD_SIZE
            att_buf[:, at : at + HEAD_SIZE] = attention[head * tokens : (head + 1) * tokens]
    weights_in.wait()
    hidden = residual_ref[...].astype(jnp.float32) + jnp.dot(
        att_buf[...], weight_buf[...], preferred_element_type=jnp.float32
    )
    hidden_ref[...] = hidden
    width = hidden.shape[1]
    normed = (
        hidden
        * lax.rsqrt(jnp.mean(hidden * hidden, axis=-1, keepdims=True) + NORM_EPSILON)
        * gain_ref[...]
    )
    rows_ref[:, :width] = normed.astype(jnp.bfloat16)
    gates = gates_ref[...]
    mixing = gates / jnp.sum(gates, axis=1, keepdims=True)
    lane = lax.broadcasted_iota(jnp.int32, (tokens, LANES), 1)
    spread = jnp.zeros((tokens, LANES), jnp.float32)
    for choice in range(TOPE):
        expert = experts_ref[:, choice : choice + 1]
        hit = jnp.logical_or(lane == expert, lane == expert + LOW_PART)
        spread += jnp.where(hit, mixing[:, choice : choice + 1], 0.0)
    high = spread.astype(jnp.bfloat16).astype(jnp.float32)
    rows_ref[:, width:] = jnp.where(lane < LOW_PART, high, spread - high).astype(jnp.bfloat16)
    gather.finish()


def expert_kernel(
    planes,
    rows_any,
    hidden_ref,
    gate_any,
    up_any,
    down_any,
    out_ref,
    row_buf,
    gate_buf,
    up_buf,
    down_buf,
    part_buf,
    core_out,
    core_in,
    across_out,
    across_in,
    plane_out,
    plane_in,
    local_sem,
    send_sem,
    recv_sem,
    back_send,
    back_recv,
):
    gather = Gather(planes, (row_buf,), send_sem, recv_sem)
    me, z, x, c = gather.me, gather.z, gather.x, gather.c
    tokens, width = hidden_ref.shape
    own = pltpu.make_async_copy(rows_any, row_buf.at[me], local_sem.at[0])
    own.start()
    weights_in = [
        pltpu.make_async_copy(source.at[0], target, local_sem.at[1 + i])
        for i, (source, target) in enumerate(
            ((gate_any, gate_buf), (up_any, up_buf), (down_any, down_buf))
        )
    ]
    greet(planes, z, x, c)
    own.wait()
    gather.take_column(jnp.int32(0))
    for copy in weights_in:
        copy.start()
    for copy in weights_in:
        copy.wait()

    def to_core(plane):
        return pltpu.make_async_remote_copy(
            src_ref=core_out.at[plane],
            dst_ref=core_in.at[plane],
            send_sem=back_send.at[0, plane],
            recv_sem=back_recv.at[0, plane],
            device_id={"blk": index_of(z, x, 1 - c)},
            device_id_type=MESH,
        )

    def to_across(plane):
        return pltpu.make_async_remote_copy(
            src_ref=across_out.at[plane],
            dst_ref=across_in.at[plane],
            send_sem=back_send.at[1, plane],
            recv_sem=back_recv.at[1, plane],
            device_id={"blk": index_of(z, 1 - x, c)},
            device_id_type=MESH,
        )

    def to_plane(plane, sender):
        return pltpu.make_async_remote_copy(
            src_ref=plane_out.at[plane],
            dst_ref=plane_in.at[sender],
            send_sem=back_send.at[2, plane],
            recv_sem=back_recv.at[2, sender],
            device_id={"blk": index_of(plane, x, c)},
            device_id_type=MESH,
        )

    @pl.loop(1, planes + 4)
    def _(k):
        @pl.when(k < planes)
        def _():
            gather.take_column(k)

        @pl.when(jnp.logical_and(k >= 1, k <= planes))
        def _():
            place = k - 1
            plane = nth_plane(place, z, planes)
            gather.take_across(place)
            gather.take_partner(place, x)
            gather.take_partner(place, 1 - x)
            rows = row_buf[pl.ds(plane * 4, 4)].reshape(4 * tokens, width + LANES)
            shares = rows[:, width:].astype(jnp.float32)
            lane = lax.broadcasted_iota(jnp.int32, shares.shape, 1)
            hit = jnp.logical_or(lane == me, lane == me + LOW_PART)
            share = jnp.sum(jnp.where(hit, shares, 0.0), axis=1, keepdims=True)
            rows = rows[:, :width]
            gate_part = jnp.dot(rows, gate_buf[...], preferred_element_type=jnp.float32)
            up_part = jnp.dot(rows, up_buf[...], preferred_element_type=jnp.float32)
            inner = (gate_part / (1.0 + jnp.exp(-gate_part)) * up_part).astype(jnp.bfloat16)
            result = share * jnp.dot(inner, down_buf[...], preferred_element_type=jnp.float32)
            part_buf[pl.ds(plane * 4, 4)] = result.reshape(4, tokens, width)
            for there in range(2):
                core_out[plane, there] = part_buf[index_of(plane, there, 1 - c)].astype(
                    jnp.bfloat16
                )
            to_core(plane).start()

        @pl.when(jnp.logical_and(k >= 2, k <= planes + 1))
        def _():
            plane = nth_plane(k - 2, z, planes)
            to_core(plane).wait_recv()
            across_out[plane] = (
                part_buf[index_of(plane, 1 - x, c)]
                + core_in[plane, 1 - x].astype(jnp.float32)
            ).astype(jnp.bfloat16)
            to_across(plane).start()

        @pl.when(k >= 3)
        def _():
            @pl.when(k <= planes + 2)
            def _():
                plane = nth_plane(k - 3, z, planes)
                to_across(plane).wait_recv()
                total = (
                    part_buf[index_of(plane, x, c)]
                    + core_in[plane, x].astype(jnp.float32)
                    + across_in[plane].astype(jnp.float32)
                )
                part_buf[index_of(plane, x, c)] = total

                @pl.when(plane != z)
                def _():
                    plane_out[plane] = total.astype(jnp.bfloat16)
                    to_plane(plane, z).start()

    out = hidden_ref[...] + part_buf[me]
    part_buf[me] = out

    @pl.loop(0, planes)
    def _(plane):
        @pl.when(plane != z)
        def _():
            to_plane(z, plane).wait_recv()
            part_buf[me] += plane_in[plane].astype(jnp.float32)

    out_ref[...] = part_buf[me].astype(jnp.bfloat16)

    @pl.loop(0, planes)
    def _(plane):
        to_core(plane).wait_send()
        to_across(plane).wait_send()

        @pl.when(plane != z)
        def _():
            to_plane(plane, z).wait_send()

    gather.finish()


def gathered(
    queries,
    rotated_cache_keys,
    stored_cache_values,
    segment_new_keys,
    segment_new_values,
    block_ids,
    residual_in,
    out_weight,
    norm_gain,
    expert_ids,
    gate_scores,
    w_gate,
    w_up,
    w_down,
):
    parties = lax.axis_size("blk")
    planes = parties // 4
    tokens, width = residual_in.shape
    bf16, f32 = jnp.bfloat16, jnp.float32
    chunks = 4
    chunk_rows = tokens * QUERY_HEADS // chunks
    inside = pl.BlockSpec(memory_space=pltpu.VMEM)
    outside = pl.BlockSpec(memory_space=pl.ANY)
    hidden, rows = pl.pallas_call(
        functools.partial(attention_kernel, planes),
        out_shape=(
            jax.ShapeDtypeStruct((tokens, width), f32),
            jax.ShapeDtypeStruct((tokens, width + LANES), bf16),
        ),
        in_specs=[inside, outside, outside] + [inside] * 4 + [outside] + [inside] * 3,
        out_specs=(inside, inside),
        scratch_shapes=[
            pltpu.VMEM((parties,) + rotated_cache_keys.shape, bf16),
            pltpu.VMEM((parties,) + stored_cache_values.shape, bf16),
            pltpu.VMEM(out_weight.shape, bf16),
            pltpu.VMEM((chunks, chunk_rows, HEAD_SIZE), bf16),
            pltpu.VMEM((tokens, QUERY_HEADS * HEAD_SIZE), bf16),
            pltpu.VMEM((chunks, chunk_rows, 1), f32),
            pltpu.VMEM((chunks, chunk_rows, 1), f32),
            pltpu.VMEM((chunks, chunk_rows, HEAD_SIZE), f32),
            pltpu.SemaphoreType.DMA((3,)),
            pltpu.SemaphoreType.DMA((2, 4, parties)),
            pltpu.SemaphoreType.DMA((2, parties)),
        ],
        compiler_params=pltpu.CompilerParams(
            collective_id=0, has_side_effects=True, vmem_limit_bytes=48 << 20
        ),
        name="attention",
    )(
        queries,
        rotated_cache_keys,
        stored_cache_values,
        segment_new_keys,
        segment_new_values,
        block_ids,
        residual_in,
        out_weight,
        norm_gain[None, :],
        expert_ids,
        gate_scores,
    )
    back = (planes, tokens, width)
    return pl.pallas_call(
        functools.partial(expert_kernel, planes),
        out_shape=jax.ShapeDtypeStruct((tokens, width), bf16),
        in_specs=[outside, inside, outside, outside, outside],
        out_specs=inside,
        scratch_shapes=[
            pltpu.VMEM((parties, tokens, width + LANES), bf16),
            pltpu.VMEM(w_gate.shape[1:], bf16),
            pltpu.VMEM(w_up.shape[1:], bf16),
            pltpu.VMEM(w_down.shape[1:], bf16),
            pltpu.VMEM((parties, tokens, width), f32),
            pltpu.VMEM((planes, 2, tokens, width), bf16),
            pltpu.VMEM((planes, 2, tokens, width), bf16),
            pltpu.VMEM(back, bf16),
            pltpu.VMEM(back, bf16),
            pltpu.VMEM(back, bf16),
            pltpu.VMEM(back, bf16),
            pltpu.SemaphoreType.DMA((4,)),
            pltpu.SemaphoreType.DMA((1, 4, parties)),
            pltpu.SemaphoreType.DMA((1, parties)),
            pltpu.SemaphoreType.DMA((3, planes)),
            pltpu.SemaphoreType.DMA((3, planes)),
        ],
        compiler_params=pltpu.CompilerParams(
            collective_id=1, has_side_effects=True, vmem_limit_bytes=48 << 20
        ),
        name="experts",
    )(rows, hidden, w_gate, w_up, w_down)


GATHER_LIMIT_BYTES = 24 << 20


def layer(*operands):
    parties = lax.axis_size("blk")
    keys, values = operands[1], operands[2]
    cache_bytes = parties * (keys.size + values.size) * keys.dtype.itemsize
    fits = cache_bytes <= GATHER_LIMIT_BYTES and parties % 4 == 0 and parties <= LOW_PART
    return gathered(*operands) if fits else body(*operands)


def solution(mesh):
    placed = (
        P(("groups", "blk"), None),
        P(("groups", "blk"), None),
        P(("groups", "blk"), None),
        P(("groups", "blk"), None),
        P(("groups", "blk"), None),
        P(("groups", "blk"), None),
        P(("groups", "blk"), None),
        P(),
        P(),
        P(("groups", "blk"), None),
        P(("groups", "blk"), None),
        P("blk", None, None),
        P("blk", None, None),
        P("blk", None, None),
    )
    return jax.shard_map(
        layer, mesh=mesh, in_specs=placed, out_specs=P(("groups", "blk"), None), check_vma=False
    )
```

```python
import functools

import jax
import jax.numpy as jnp
from jax import lax
from jax.experimental import pallas as pl
from jax.experimental.pallas import tpu as pltpu
from jax.sharding import PartitionSpec as P

QUERY_HEADS = 16
KEY_VALUE_HEADS = 2
HEAD_SIZE = 128
TOPB = 8
TOPE = 8


NORM_EPSILON = 1e-06


def partials(query_rows, key_rows, value_rows, causal):
    queries_per_cluster = QUERY_HEADS // KEY_VALUE_HEADS
    score_scale = HEAD_SIZE ** (-0.5)
    maxima = []
    totals = []
    outputs = []
    for head_cluster in range(KEY_VALUE_HEADS):
        offset = head_cluster * queries_per_cluster * HEAD_SIZE
        group_queries = query_rows[:, offset : offset + queries_per_cluster * HEAD_SIZE].reshape(
            -1, HEAD_SIZE
        )
        group_keys = key_rows[:, head_cluster * HEAD_SIZE : (head_cluster + 1) * HEAD_SIZE]
        group_values = value_rows[:, head_cluster * HEAD_SIZE : (head_cluster + 1) * HEAD_SIZE]
        scores = (
            lax.dot_general(
                group_queries,
                group_keys,
                (((1,), (1,)), ((), ())),
                preferred_element_type=jnp.float32,
            )
            * score_scale
        )
        if causal:
            owner_row = jnp.arange(group_queries.shape[0], dtype=jnp.int32) // queries_per_cluster
            key_place = jnp.arange(key_rows.shape[0], dtype=jnp.int32)
            scores = jnp.where(key_place[None, :] <= owner_row[:, None], scores, -jnp.inf)
        row_max = jnp.max(scores, axis=1)
        weights = jnp.exp(scores - row_max[:, None])
        maxima.append(row_max.reshape(-1, queries_per_cluster))
        totals.append(jnp.sum(weights, axis=1).reshape(-1, queries_per_cluster))
        mixed_rows = jnp.dot(
            weights.astype(jnp.bfloat16), group_values, preferred_element_type=jnp.float32
        )
        outputs.append(mixed_rows.reshape(-1, queries_per_cluster * HEAD_SIZE))
    return (
        jnp.concatenate(maxima, axis=1),
        jnp.concatenate(totals, axis=1),
        jnp.concatenate(outputs, axis=1),
    )


def bucket_slots(targets, capacity, parties):
    flat_targets = targets.reshape(-1)
    pair_count = flat_targets.shape[0]
    one_hot = (flat_targets[:, None] == jnp.arange(parties, dtype=jnp.int32)[None, :]).astype(
        jnp.int32
    )
    before = jnp.sum((jnp.cumsum(one_hot, axis=0) - one_hot) * one_hot, axis=1)
    slot_index = flat_targets * capacity + before
    filler = (
        jnp.full((parties * capacity,), pair_count, jnp.int32)
        .at[slot_index]
        .set(jnp.arange(pair_count, dtype=jnp.int32))
    )
    return (slot_index, filler)


def body(
    queries,
    rotated_cache_keys,
    stored_cache_values,
    segment_new_keys,
    segment_new_values,
    block_ids,
    residual_in,
    out_weight,
    norm_gain,
    expert_ids,
    gate_scores,
    w_gate,
    w_up,
    w_down,
):
    parties = lax.axis_size("blk")
    tok_count = queries.shape[0]
    capacity = tok_count * TOPB * 5 // (4 * parties)
    expert_capacity = tok_count * TOPE * 3 // (2 * parties)
    owner_slots, slot_pair = bucket_slots(block_ids, capacity, parties)
    pair_count = tok_count * TOPB
    occupied = slot_pair < pair_count
    source_token = jnp.minimum(slot_pair, pair_count - 1) // TOPB
    outgoing = jnp.where(
        occupied[:, None], queries[source_token], jnp.zeros((), queries.dtype)
    ).reshape(parties, capacity, QUERY_HEADS * HEAD_SIZE)
    arrived = lax.all_to_all(outgoing, "blk", split_axis=0, concat_axis=0, tiled=True)
    senders, items, row_width = arrived.shape
    far_max, far_total, far_out = partials(
        arrived.reshape(senders * items, row_width), rotated_cache_keys, stored_cache_values, False
    )
    back_max = lax.all_to_all(
        far_max.reshape(senders, items, QUERY_HEADS), "blk", split_axis=0, concat_axis=0, tiled=True
    )
    back_total = lax.all_to_all(
        far_total.reshape(senders, items, QUERY_HEADS),
        "blk",
        split_axis=0,
        concat_axis=0,
        tiled=True,
    )
    back_out = lax.all_to_all(
        far_out.astype(jnp.bfloat16).reshape(senders, items, row_width),
        "blk",
        split_axis=0,
        concat_axis=0,
        tiled=True,
    )
    local_row_maximum, local_denominator, local_output = partials(
        queries, segment_new_keys, segment_new_values, True
    )
    pair_max = back_max.reshape(-1, QUERY_HEADS)[owner_slots].reshape(tok_count, TOPB, QUERY_HEADS)
    pair_total = back_total.reshape(-1, QUERY_HEADS)[owner_slots].reshape(
        tok_count, TOPB, QUERY_HEADS
    )
    pair_out = back_out.reshape(-1, QUERY_HEADS * HEAD_SIZE)[owner_slots].reshape(
        tok_count, TOPB, QUERY_HEADS, HEAD_SIZE
    )
    ceiling = jnp.maximum(local_row_maximum, jnp.max(pair_max, axis=1))
    own_scale = jnp.exp(local_row_maximum - ceiling)
    pair_scale = jnp.exp(pair_max - ceiling[:, None, :])
    denominator = local_denominator * own_scale + jnp.sum(pair_total * pair_scale, axis=1)
    numerator = local_output.reshape(tok_count, QUERY_HEADS, HEAD_SIZE) * own_scale[
        :, :, None
    ] + jnp.einsum("tjh,tjhd->thd", pair_scale, pair_out, preferred_element_type=jnp.float32)
    attention = (
        (numerator / denominator[:, :, None])
        .reshape(tok_count, QUERY_HEADS * HEAD_SIZE)
        .astype(jnp.bfloat16)
    )
    hidden_state = residual_in.astype(jnp.float32) + jnp.dot(
        attention, out_weight, preferred_element_type=jnp.float32
    )
    normed = (
        hidden_state
        * lax.rsqrt(jnp.mean(hidden_state * hidden_state, axis=-1, keepdims=True) + NORM_EPSILON)
        * norm_gain
    ).astype(jnp.bfloat16)
    expert_slots, expert_pair = bucket_slots(expert_ids, expert_capacity, parties)
    expert_pairs = tok_count * TOPE
    expert_used = expert_pair < expert_pairs
    expert_token = jnp.minimum(expert_pair, expert_pairs - 1) // TOPE
    dispatched = jnp.where(
        expert_used[:, None], normed[expert_token], jnp.zeros((), normed.dtype)
    ).reshape(parties, expert_capacity, normed.shape[1])
    arrived = lax.all_to_all(dispatched, "blk", split_axis=0, concat_axis=0, tiled=True)
    flat_rows = arrived.reshape(-1, arrived.shape[2])
    gate_part = jnp.dot(flat_rows, w_gate[0], preferred_element_type=jnp.float32)
    up_part = jnp.dot(flat_rows, w_up[0], preferred_element_type=jnp.float32)
    inner = (jax.nn.silu(gate_part) * up_part).astype(jnp.bfloat16)
    expert_out = (
        jnp.dot(inner, w_down[0], preferred_element_type=jnp.float32)
        .astype(jnp.bfloat16)
        .reshape(arrived.shape)
    )
    returned = lax.all_to_all(expert_out, "blk", split_axis=0, concat_axis=0, tiled=True)
    gathered_rows = returned.reshape(-1, normed.shape[1])[expert_slots].reshape(
        tok_count, TOPE, normed.shape[1]
    )
    mixing = gate_scores / jnp.sum(gate_scores, axis=1, keepdims=True)
    mixture = jnp.einsum("tk,tkd->td", mixing, gathered_rows, preferred_element_type=jnp.float32)
    return (hidden_state + mixture).astype(jnp.bfloat16)


LANES = 128
LOW_PART = 64
MESH = pl.DeviceIdType.MESH
LOG2_E = 1.4426950408889634


def place_of(index):
    return lax.div(index, 4), lax.rem(lax.div(index, 2), 2), lax.rem(index, 2)


def index_of(z, x, c):
    return (z * 2 + x) * 2 + c


def nth_plane(k, z, planes):
    low = jnp.minimum(z, planes - 1 - z)
    near = k <= 2 * low
    far = jnp.where(near, lax.div(k + 1, 2), k - low)
    up = jnp.where(near, lax.rem(k, 2), (z < planes - 1 - z).astype(jnp.int32))
    return z + far * (2 * up - 1)


class Gather:
    def __init__(self, planes, parts, send_sem, recv_sem):
        self.planes, self.parts, self.send_sem, self.recv_sem = planes, parts, send_sem, recv_sem
        self.me = lax.axis_index("blk")
        self.z, self.x, self.c = place_of(self.me)

    def copy(self, part, way, block):
        z, x, c = self.z, self.x, self.c
        target = (
            index_of(z + 1, x, c),
            index_of(z - 1, x, c),
            index_of(z, 1 - x, c),
            index_of(z, x, 1 - c),
        )[way]
        buf, first, rows, _ = self.parts[part]
        piece = buf.at[block, first : first + rows]
        return pltpu.make_async_remote_copy(
            src_ref=piece,
            dst_ref=piece,
            send_sem=self.send_sem.at[part, way, block],
            recv_sem=self.recv_sem.at[part, block],
            device_id={"blk": target},
            device_id_type=MESH,
        )

    def across_first(self, part):
        return self.parts[part][3]

    def arrive(self, part, block):
        self.copy(part, 3, block).wait_recv()

    def along_z(self, part, plane, block, act):
        up = jnp.logical_and(plane <= self.z, self.z < self.planes - 1)
        down = jnp.logical_and(plane >= self.z, self.z > 0)

        @pl.when(up)
        def _():
            act(self.copy(part, 0, block))

        @pl.when(down)
        def _():
            act(self.copy(part, 1, block))

    def start(self):
        for part in range(len(self.parts)):
            for way in (2, 3):
                self.copy(part, way, self.me).start()
            self.along_z(part, self.z, self.me, lambda copy: copy.start())

    def take_first_across(self):
        block = index_of(self.z, 1 - self.x, self.c)
        for part in range(len(self.parts)):
            if self.across_first(part):
                self.arrive(part, block)
                self.along_z(part, self.z, block, lambda copy: copy.start())
                self.copy(part, 3, block).start()

    def take_column(self, k):
        plane = nth_plane(k, self.z, self.planes)
        block = index_of(plane, self.x, self.c)
        across = index_of(plane, 1 - self.x, self.c)
        for part in range(len(self.parts)):
            self.arrive(part, block)
            self.along_z(part, plane, block, lambda copy: copy.start())
            if not self.across_first(part):
                self.copy(part, 2, block).start()
            self.copy(part, 3, block).start()
        for part in range(len(self.parts)):
            if self.across_first(part):
                self.arrive(part, across)
                self.along_z(part, plane, across, lambda copy: copy.start())
                self.copy(part, 3, across).start()

    def take_across(self, k):
        plane = nth_plane(k, self.z, self.planes)
        block = index_of(plane, 1 - self.x, self.c)
        for part in range(len(self.parts)):
            if not self.across_first(part):
                self.arrive(part, block)
                self.copy(part, 3, block).start()

    def take_partner(self, k, x):
        plane = nth_plane(k, self.z, self.planes)
        for part in range(len(self.parts)):
            self.arrive(part, index_of(plane, x, 1 - self.c))

    def finish(self):
        @pl.loop(0, self.planes)
        def _(plane):
            block = index_of(plane, self.x, self.c)
            across = index_of(plane, 1 - self.x, self.c)
            for part in range(len(self.parts)):
                self.along_z(part, plane, block, lambda copy: copy.wait_send())
                self.copy(part, 3, block).wait_send()
                self.copy(part, 3, across).wait_send()
                if self.across_first(part):
                    self.along_z(part, plane, across, lambda copy: copy.wait_send())
                else:
                    self.copy(part, 2, block).wait_send()
            for part in range(len(self.parts)):
                if self.across_first(part):

                    @pl.when(plane == self.z)
                    def _():
                        self.copy(part, 2, block).wait_send()


def greet(planes, z, x, c):
    barrier = pltpu.get_barrier_semaphore()
    for target in (index_of(z, 1 - x, c), index_of(z, x, 1 - c)):
        pl.semaphore_signal(barrier, inc=1, device_id={"blk": target}, device_id_type=MESH)

    @pl.loop(0, planes)
    def _(plane):
        @pl.when(plane != z)
        def _():
            pl.semaphore_signal(
                barrier, inc=1, device_id={"blk": index_of(plane, x, c)}, device_id_type=MESH
            )

    pl.semaphore_wait(barrier, planes + 1)


def columns_of(rows, tokens):
    down = lax.broadcasted_iota(jnp.int32, (tokens, tokens), 0)
    right = lax.broadcasted_iota(jnp.int32, (tokens, tokens), 1)
    return [
        jnp.sum(jnp.where(down == right, rows[i : i + 1, :], 0.0), axis=1, keepdims=True)
        for i in range(rows.shape[0])
    ]


def layer_kernel(
    planes,
    cut_keys,
    cut_rows,
    q_any,
    k_any,
    v_any,
    new_k_any,
    new_v_any,
    ids_any,
    residual_any,
    weight_any,
    gain_any,
    experts_any,
    gates_any,
    gate_any,
    up_any,
    down_any,
    out_ref,
    kv_buf,
    q_in,
    new_k_ref,
    new_v_ref,
    ids_in,
    residual_ref,
    weight_buf,
    gain_ref,
    experts_in,
    gates_in,
    gate_buf,
    up_buf,
    down_buf,
    ids_ref,
    q_buf,
    att_buf,
    max_buf,
    sum_buf,
    acc_buf,
    hidden_ref,
    row_buf,
    part_buf,
    core_out,
    core_in,
    across_out,
    across_in,
    plane_out,
    plane_in,
    local_sem,
    send_sem,
    recv_sem,
    row_send_sem,
    row_recv_sem,
    back_send,
    back_recv,
):
    keys = k_any.shape[0]
    low, high = keys - cut_keys, keys + cut_keys
    gather = Gather(
        planes,
        (
            (kv_buf, low, 2 * cut_keys, True),
            (kv_buf, 0, low, False),
            (kv_buf, high, keys - cut_keys, False),
        ),
        send_sem,
        recv_sem,
    )
    tokens, width = residual_ref.shape
    row_parts = ((row_buf, cut_rows, tokens - cut_rows, False),)
    if cut_rows:
        row_parts = ((row_buf, 0, cut_rows, True),) + row_parts
    row_gather = Gather(planes, row_parts, row_send_sem, row_recv_sem)
    me, z, x, c = gather.me, gather.z, gather.x, gather.c
    moves = (
        (k_any, kv_buf.at[me, 0:keys]),
        (v_any, kv_buf.at[me, keys : 2 * keys]),
        (q_any, q_in),
        (new_k_any, new_k_ref),
        (new_v_any, new_v_ref),
        (ids_any, ids_in),
        (experts_any, experts_in),
        (gates_any, gates_in),
        (residual_any, residual_ref),
        (gain_any, gain_ref),
        (weight_any, weight_buf),
        (gate_any.at[0], gate_buf),
        (up_any.at[0], up_buf),
        (down_any.at[0], down_buf),
    )
    loads = [
        pltpu.make_async_copy(source, target, local_sem.at[i])
        for i, (source, target) in enumerate(moves)
    ]
    for load in loads[:10]:
        load.start()
    greet(planes, z, x, c)
    for load in loads[:2]:
        load.wait()
    gather.start()
    for load in loads[10:]:
        load.start()
    for load in loads[2:10]:
        load.wait()

    chunks, chunk_rows, _ = q_buf.shape
    heads = chunk_rows // tokens
    chunks_per_group = chunks // KEY_VALUE_HEADS
    factor = HEAD_SIZE ** (-0.5) * LOG2_E

    lane = lax.broadcasted_iota(jnp.int32, (tokens, LANES), 1)
    ids = jnp.full((tokens, LANES), -1.0, jnp.float32)
    for choice, column in enumerate(columns_of(ids_in[...].astype(jnp.float32), tokens)):
        ids = jnp.where(lane == choice, column, ids)
    ids_ref[...] = ids

    for chunk in range(chunks):
        group = chunk // chunks_per_group
        lanes = slice(group * HEAD_SIZE, (group + 1) * HEAD_SIZE)
        for head in range(heads):
            at = (chunk * heads + head) * HEAD_SIZE
            q_buf[chunk, head * tokens : (head + 1) * tokens, :] = q_in[:, at : at + HEAD_SIZE]
        scores = lax.dot_general(
            q_buf[chunk],
            new_k_ref[:, lanes],
            (((1,), (1,)), ((), ())),
            preferred_element_type=jnp.float32,
        )
        row = lax.rem(lax.broadcasted_iota(jnp.int32, scores.shape, 0), tokens)
        key = lax.broadcasted_iota(jnp.int32, scores.shape, 1)
        scores = jnp.where(key <= row, scores, -jnp.inf)
        top = jnp.max(scores, axis=1, keepdims=True)
        weights = jnp.exp2((scores - top) * factor)
        max_buf[chunk] = top
        sum_buf[chunk] = jnp.sum(weights, axis=1, keepdims=True)
        acc_buf[chunk] = jnp.dot(
            weights.astype(jnp.bfloat16), new_v_ref[:, lanes], preferred_element_type=jnp.float32
        )
    gather.take_first_across()

    @pl.loop(0, 4 * (planes + 1))
    def _(step):
        k, kind = lax.div(step, 4), lax.rem(step, 4)
        late = lax.div(kind, 2)
        valid = jnp.logical_or(
            jnp.logical_and(late == 0, k < planes), jnp.logical_and(late == 1, k > 0)
        )

        @pl.when(valid)
        def _():
            place = k - late
            plane = nth_plane(place, z, planes)

            @pl.when(jnp.logical_and(kind == 0, k > 0))
            def _():
                gather.take_column(k)

            @pl.when(kind == 1)
            def _():
                gather.take_partner(place, x)

            @pl.when(kind == 2)
            def _():
                gather.take_across(place)

            @pl.when(kind == 3)
            def _():
                gather.take_partner(place, 1 - x)

            other_core = lax.rem(kind, 2)
            block = index_of(
                plane,
                x + late * (1 - 2 * x),
                c + other_core * (1 - 2 * c),
            )
            named = jnp.sum(
                jnp.where(ids_ref[...] == block.astype(jnp.float32), 1.0, 0.0),
                axis=1,
                keepdims=True,
            )
            named = jnp.concatenate([named] * heads, axis=0) > 0.5
            for chunk in range(chunks):
                group = chunk // chunks_per_group
                lanes = slice(group * HEAD_SIZE, (group + 1) * HEAD_SIZE)
                scores = lax.dot_general(
                    q_buf[chunk],
                    kv_buf[block, 0:keys, lanes],
                    (((1,), (1,)), ((), ())),
                    preferred_element_type=jnp.float32,
                )
                before = max_buf[chunk]
                top = jnp.maximum(before, jnp.max(scores, axis=1, keepdims=True))
                weights = jnp.exp2((scores - top) * factor)
                scale = jnp.where(named, jnp.exp2((before - top) * factor), 1.0)
                total = jnp.sum(weights, axis=1, keepdims=True)
                mixed = jnp.dot(
                    weights.astype(jnp.bfloat16),
                    kv_buf[block, keys : 2 * keys, lanes],
                    preferred_element_type=jnp.float32,
                )
                max_buf[chunk] = jnp.where(named, top, before)
                sum_buf[chunk] = sum_buf[chunk] * scale + jnp.where(named, total, 0.0)
                acc_buf[chunk] = acc_buf[chunk] * scale + jnp.where(named, mixed, 0.0)

            @pl.when(step == 0)
            def _():
                gates = gates_in[...]
                mixing = gates / jnp.sum(gates, axis=0, keepdims=True)
                spread = jnp.zeros((tokens, LANES), jnp.float32)
                columns = zip(
                    columns_of(experts_in[...].astype(jnp.float32), tokens),
                    columns_of(mixing, tokens),
                )
                for expert, share in columns:
                    expert = expert.astype(jnp.int32)
                    hit = jnp.logical_or(lane == expert, lane == expert + LOW_PART)
                    spread += jnp.where(hit, share, 0.0)
                rounded = spread.astype(jnp.bfloat16).astype(jnp.float32)
                row_buf[me, :, width:] = jnp.where(
                    lane < LOW_PART, rounded, spread - rounded
                ).astype(jnp.bfloat16)

    for chunk in range(chunks):
        attention = (acc_buf[chunk] / sum_buf[chunk]).astype(jnp.bfloat16)
        for head in range(heads):
            at = (chunk * heads + head) * HEAD_SIZE
            att_buf[:, at : at + HEAD_SIZE] = attention[head * tokens : (head + 1) * tokens]
    for load in loads[10:]:
        load.wait()
    hidden = residual_ref[...].astype(jnp.float32) + jnp.dot(
        att_buf[...], weight_buf[...], preferred_element_type=jnp.float32
    )
    normed = (
        hidden
        * lax.rsqrt(jnp.mean(hidden * hidden, axis=-1, keepdims=True) + NORM_EPSILON)
        * gain_ref[...]
    )
    row_buf[me, :, :width] = normed.astype(jnp.bfloat16)
    row_gather.start()
    halves = core_out.shape[1]
    half_width = width // halves

    def cols(half):
        return slice(half * half_width, (half + 1) * half_width)

    def to_core(plane, half):
        return pltpu.make_async_remote_copy(
            src_ref=core_out.at[plane, half],
            dst_ref=core_in.at[plane, half],
            send_sem=back_send.at[0, plane, half],
            recv_sem=back_recv.at[0, plane, half],
            device_id={"blk": index_of(z, x, 1 - c)},
            device_id_type=MESH,
        )

    def to_across(plane, half):
        return pltpu.make_async_remote_copy(
            src_ref=across_out.at[plane, half],
            dst_ref=across_in.at[plane, half],
            send_sem=back_send.at[1, plane, half],
            recv_sem=back_recv.at[1, plane, half],
            device_id={"blk": index_of(z, 1 - x, c)},
            device_id_type=MESH,
        )

    def to_plane(plane, half, sender):
        return pltpu.make_async_remote_copy(
            src_ref=plane_out.at[plane, half],
            dst_ref=plane_in.at[sender, half],
            send_sem=back_send.at[2, plane, half],
            recv_sem=back_recv.at[2, sender, half],
            device_id={"blk": index_of(plane, x, c)},
            device_id_type=MESH,
        )

    hidden_ref[...] = hidden
    row_gather.take_first_across()

    @pl.loop(1, planes + 3)
    def _(k):
        @pl.when(k < planes)
        def _():
            row_gather.take_column(k)

        @pl.when(k <= planes)
        def _():
            place = k - 1
            plane = nth_plane(place, z, planes)
            row_gather.take_across(place)
            row_gather.take_partner(place, x)
            row_gather.take_partner(place, 1 - x)
            rows = row_buf[pl.ds(plane * 4, 4)].reshape(4 * tokens, width + LANES)
            shares = rows[:, width:].astype(jnp.float32)
            place_lane = lax.broadcasted_iota(jnp.int32, shares.shape, 1)
            hit = jnp.logical_or(place_lane == me, place_lane == me + LOW_PART)
            share = jnp.sum(jnp.where(hit, shares, 0.0), axis=1, keepdims=True)
            rows = rows[:, :width]
            gate_part = jnp.dot(rows, gate_buf[...], preferred_element_type=jnp.float32)
            up_part = jnp.dot(rows, up_buf[...], preferred_element_type=jnp.float32)
            inner = (gate_part / (1.0 + jnp.exp(-gate_part)) * up_part).astype(jnp.bfloat16)
            for half in range(halves):
                result = share * jnp.dot(
                    inner, down_buf[:, cols(half)], preferred_element_type=jnp.float32
                )
                part_buf[pl.ds(plane * 4, 4), :, cols(half)] = result.reshape(
                    4, tokens, half_width
                )
                for there in range(2):
                    core_out[plane, half, there] = part_buf[
                        index_of(plane, there, 1 - c), :, cols(half)
                    ].astype(jnp.bfloat16)
                to_core(plane, half).start()

        @pl.when(jnp.logical_and(k >= 2, k <= planes + 1))
        def _():
            plane = nth_plane(k - 2, z, planes)
            for half in range(halves):
                to_core(plane, half).wait_recv()
                across_out[plane, half] = (
                    part_buf[index_of(plane, 1 - x, c), :, cols(half)]
                    + core_in[plane, half, 1 - x].astype(jnp.float32)
                ).astype(jnp.bfloat16)
                to_across(plane, half).start()

        @pl.when(k >= 3)
        def _():
            plane = nth_plane(k - 3, z, planes)
            for half in range(halves):
                to_across(plane, half).wait_recv()
                total = (
                    part_buf[index_of(plane, x, c), :, cols(half)]
                    + core_in[plane, half, x].astype(jnp.float32)
                    + across_in[plane, half].astype(jnp.float32)
                )
                part_buf[index_of(plane, x, c), :, cols(half)] = total

                @pl.when(plane != z)
                def _():
                    plane_out[plane, half] = total.astype(jnp.bfloat16)
                    to_plane(plane, half, z).start()

    part_buf[me] += hidden_ref[...]

    @pl.loop(0, planes)
    def _(plane):
        @pl.when(plane != z)
        def _():
            for half in range(halves):
                to_plane(z, half, plane).wait_recv()
                part_buf[me, :, cols(half)] += plane_in[plane, half].astype(jnp.float32)

    out_ref[...] = part_buf[me].astype(jnp.bfloat16)

    @pl.loop(0, planes)
    def _(plane):
        for half in range(halves):
            to_core(plane, half).wait_send()
            to_across(plane, half).wait_send()

            @pl.when(plane != z)
            def _():
                to_plane(plane, half, z).wait_send()

    gather.finish()
    row_gather.finish()


def gathered(*operands):
    (
        queries,
        cache_keys,
        cache_values,
        new_keys,
        new_values,
        block_ids,
        residual,
        out_weight,
        norm_gain,
        expert_ids,
        gate_scores,
        w_gate,
        w_up,
        w_down,
    ) = operands
    parties = lax.axis_size("blk")
    planes = parties // 4
    tokens, width = residual.shape
    keys, lanes = cache_keys.shape
    bf16, f32 = jnp.bfloat16, jnp.float32
    chunks, halves = 4, 2
    chunk_rows = tokens * QUERY_HEADS // chunks
    cut_keys = keys * 5 // 32 // 16 * 16
    cut_rows = tokens // 4 // 16 * 16
    outside = pl.BlockSpec(memory_space=pltpu.HBM)
    inputs = (
        queries,
        cache_keys,
        cache_values,
        new_keys,
        new_values,
        block_ids.T,
        residual,
        out_weight,
        norm_gain[None, :],
        expert_ids.T,
        gate_scores.T,
        w_gate,
        w_up,
        w_down,
    )

    def like(array):
        return pltpu.VMEM(array.shape, array.dtype)

    back = (planes, halves, tokens, width // halves)
    core_back = (planes, halves, 2, tokens, width // halves)
    row_parts = 2 if cut_rows else 1
    return pl.pallas_call(
        functools.partial(layer_kernel, planes, cut_keys, cut_rows),
        out_shape=jax.ShapeDtypeStruct((tokens, width), bf16),
        in_specs=[outside] * len(inputs),
        out_specs=pl.BlockSpec(memory_space=pltpu.VMEM),
        scratch_shapes=[
            pltpu.VMEM((parties, 2 * keys, lanes), bf16),
            like(inputs[0]),
            like(inputs[3]),
            like(inputs[4]),
            like(inputs[5]),
            like(inputs[6]),
            like(inputs[7]),
            like(inputs[8]),
            like(inputs[9]),
            like(inputs[10]),
            pltpu.VMEM(w_gate.shape[1:], bf16),
            pltpu.VMEM(w_up.shape[1:], bf16),
            pltpu.VMEM(w_down.shape[1:], bf16),
            pltpu.VMEM((tokens, LANES), f32),
            pltpu.VMEM((chunks, chunk_rows, HEAD_SIZE), bf16),
            pltpu.VMEM((tokens, QUERY_HEADS * HEAD_SIZE), bf16),
            pltpu.VMEM((chunks, chunk_rows, 1), f32),
            pltpu.VMEM((chunks, chunk_rows, 1), f32),
            pltpu.VMEM((chunks, chunk_rows, HEAD_SIZE), f32),
            pltpu.VMEM((tokens, width), f32),
            pltpu.VMEM((parties, tokens, width + LANES), bf16),
            pltpu.VMEM((parties, tokens, width), f32),
            pltpu.VMEM(core_back, bf16),
            pltpu.VMEM(core_back, bf16),
            pltpu.VMEM(back, bf16),
            pltpu.VMEM(back, bf16),
            pltpu.VMEM(back, bf16),
            pltpu.VMEM(back, bf16),
            pltpu.SemaphoreType.DMA((14,)),
            pltpu.SemaphoreType.DMA((3, 4, parties)),
            pltpu.SemaphoreType.DMA((3, parties)),
            pltpu.SemaphoreType.DMA((row_parts, 4, parties)),
            pltpu.SemaphoreType.DMA((row_parts, parties)),
            pltpu.SemaphoreType.DMA((3, planes, halves)),
            pltpu.SemaphoreType.DMA((3, planes, halves)),
        ],
        compiler_params=pltpu.CompilerParams(
            collective_id=0, has_side_effects=True, vmem_limit_bytes=60 << 20
        ),
        name="layer",
    )(*inputs)


GATHER_LIMIT_BYTES = 24 << 20


def layer(*operands):
    parties = lax.axis_size("blk")
    keys, values = operands[1], operands[2]
    cache_bytes = parties * (keys.size + values.size) * keys.dtype.itemsize
    fits = cache_bytes <= GATHER_LIMIT_BYTES and parties % 4 == 0 and parties <= LOW_PART
    return gathered(*operands) if fits else body(*operands)


def solution(mesh):
    placed = (
        P(("groups", "blk"), None),
        P(("groups", "blk"), None),
        P(("groups", "blk"), None),
        P(("groups", "blk"), None),
        P(("groups", "blk"), None),
        P(("groups", "blk"), None),
        P(("groups", "blk"), None),
        P(),
        P(),
        P(("groups", "blk"), None),
        P(("groups", "blk"), None),
        P("blk", None, None),
        P("blk", None, None),
        P("blk", None, None),
    )
    return jax.shard_map(
        layer, mesh=mesh, in_specs=placed, out_specs=P(("groups", "blk"), None), check_vma=False
    )
```

```python
import functools

import jax
import jax.numpy as jnp
from jax import lax
from jax.experimental import pallas as pl
from jax.experimental.pallas import tpu as pltpu
from jax.sharding import PartitionSpec as P

QUERY_HEADS = 16
KEY_VALUE_HEADS = 2
HEAD_SIZE = 128
TOPB = 8
TOPE = 8


NORM_EPSILON = 1e-06


def partials(query_rows, key_rows, value_rows, causal):
    queries_per_cluster = QUERY_HEADS // KEY_VALUE_HEADS
    score_scale = HEAD_SIZE ** (-0.5)
    maxima = []
    totals = []
    outputs = []
    for head_cluster in range(KEY_VALUE_HEADS):
        offset = head_cluster * queries_per_cluster * HEAD_SIZE
        group_queries = query_rows[:, offset : offset + queries_per_cluster * HEAD_SIZE].reshape(
            -1, HEAD_SIZE
        )
        group_keys = key_rows[:, head_cluster * HEAD_SIZE : (head_cluster + 1) * HEAD_SIZE]
        group_values = value_rows[:, head_cluster * HEAD_SIZE : (head_cluster + 1) * HEAD_SIZE]
        scores = (
            lax.dot_general(
                group_queries,
                group_keys,
                (((1,), (1,)), ((), ())),
                preferred_element_type=jnp.float32,
            )
            * score_scale
        )
        if causal:
            owner_row = jnp.arange(group_queries.shape[0], dtype=jnp.int32) // queries_per_cluster
            key_place = jnp.arange(key_rows.shape[0], dtype=jnp.int32)
            scores = jnp.where(key_place[None, :] <= owner_row[:, None], scores, -jnp.inf)
        row_max = jnp.max(scores, axis=1)
        weights = jnp.exp(scores - row_max[:, None])
        maxima.append(row_max.reshape(-1, queries_per_cluster))
        totals.append(jnp.sum(weights, axis=1).reshape(-1, queries_per_cluster))
        mixed_rows = jnp.dot(
            weights.astype(jnp.bfloat16), group_values, preferred_element_type=jnp.float32
        )
        outputs.append(mixed_rows.reshape(-1, queries_per_cluster * HEAD_SIZE))
    return (
        jnp.concatenate(maxima, axis=1),
        jnp.concatenate(totals, axis=1),
        jnp.concatenate(outputs, axis=1),
    )


def bucket_slots(targets, capacity, parties):
    flat_targets = targets.reshape(-1)
    pair_count = flat_targets.shape[0]
    one_hot = (flat_targets[:, None] == jnp.arange(parties, dtype=jnp.int32)[None, :]).astype(
        jnp.int32
    )
    before = jnp.sum((jnp.cumsum(one_hot, axis=0) - one_hot) * one_hot, axis=1)
    slot_index = flat_targets * capacity + before
    filler = (
        jnp.full((parties * capacity,), pair_count, jnp.int32)
        .at[slot_index]
        .set(jnp.arange(pair_count, dtype=jnp.int32))
    )
    return (slot_index, filler)


def body(
    queries,
    rotated_cache_keys,
    stored_cache_values,
    segment_new_keys,
    segment_new_values,
    block_ids,
    residual_in,
    out_weight,
    norm_gain,
    expert_ids,
    gate_scores,
    w_gate,
    w_up,
    w_down,
):
    parties = lax.axis_size("blk")
    tok_count = queries.shape[0]
    capacity = tok_count * TOPB * 5 // (4 * parties)
    expert_capacity = tok_count * TOPE * 3 // (2 * parties)
    owner_slots, slot_pair = bucket_slots(block_ids, capacity, parties)
    pair_count = tok_count * TOPB
    occupied = slot_pair < pair_count
    source_token = jnp.minimum(slot_pair, pair_count - 1) // TOPB
    outgoing = jnp.where(
        occupied[:, None], queries[source_token], jnp.zeros((), queries.dtype)
    ).reshape(parties, capacity, QUERY_HEADS * HEAD_SIZE)
    arrived = lax.all_to_all(outgoing, "blk", split_axis=0, concat_axis=0, tiled=True)
    senders, items, row_width = arrived.shape
    far_max, far_total, far_out = partials(
        arrived.reshape(senders * items, row_width), rotated_cache_keys, stored_cache_values, False
    )
    back_max = lax.all_to_all(
        far_max.reshape(senders, items, QUERY_HEADS), "blk", split_axis=0, concat_axis=0, tiled=True
    )
    back_total = lax.all_to_all(
        far_total.reshape(senders, items, QUERY_HEADS),
        "blk",
        split_axis=0,
        concat_axis=0,
        tiled=True,
    )
    back_out = lax.all_to_all(
        far_out.astype(jnp.bfloat16).reshape(senders, items, row_width),
        "blk",
        split_axis=0,
        concat_axis=0,
        tiled=True,
    )
    local_row_maximum, local_denominator, local_output = partials(
        queries, segment_new_keys, segment_new_values, True
    )
    pair_max = back_max.reshape(-1, QUERY_HEADS)[owner_slots].reshape(tok_count, TOPB, QUERY_HEADS)
    pair_total = back_total.reshape(-1, QUERY_HEADS)[owner_slots].reshape(
        tok_count, TOPB, QUERY_HEADS
    )
    pair_out = back_out.reshape(-1, QUERY_HEADS * HEAD_SIZE)[owner_slots].reshape(
        tok_count, TOPB, QUERY_HEADS, HEAD_SIZE
    )
    ceiling = jnp.maximum(local_row_maximum, jnp.max(pair_max, axis=1))
    own_scale = jnp.exp(local_row_maximum - ceiling)
    pair_scale = jnp.exp(pair_max - ceiling[:, None, :])
    denominator = local_denominator * own_scale + jnp.sum(pair_total * pair_scale, axis=1)
    numerator = local_output.reshape(tok_count, QUERY_HEADS, HEAD_SIZE) * own_scale[
        :, :, None
    ] + jnp.einsum("tjh,tjhd->thd", pair_scale, pair_out, preferred_element_type=jnp.float32)
    attention = (
        (numerator / denominator[:, :, None])
        .reshape(tok_count, QUERY_HEADS * HEAD_SIZE)
        .astype(jnp.bfloat16)
    )
    hidden_state = residual_in.astype(jnp.float32) + jnp.dot(
        attention, out_weight, preferred_element_type=jnp.float32
    )
    normed = (
        hidden_state
        * lax.rsqrt(jnp.mean(hidden_state * hidden_state, axis=-1, keepdims=True) + NORM_EPSILON)
        * norm_gain
    ).astype(jnp.bfloat16)
    expert_slots, expert_pair = bucket_slots(expert_ids, expert_capacity, parties)
    expert_pairs = tok_count * TOPE
    expert_used = expert_pair < expert_pairs
    expert_token = jnp.minimum(expert_pair, expert_pairs - 1) // TOPE
    dispatched = jnp.where(
        expert_used[:, None], normed[expert_token], jnp.zeros((), normed.dtype)
    ).reshape(parties, expert_capacity, normed.shape[1])
    arrived = lax.all_to_all(dispatched, "blk", split_axis=0, concat_axis=0, tiled=True)
    flat_rows = arrived.reshape(-1, arrived.shape[2])
    gate_part = jnp.dot(flat_rows, w_gate[0], preferred_element_type=jnp.float32)
    up_part = jnp.dot(flat_rows, w_up[0], preferred_element_type=jnp.float32)
    inner = (jax.nn.silu(gate_part) * up_part).astype(jnp.bfloat16)
    expert_out = (
        jnp.dot(inner, w_down[0], preferred_element_type=jnp.float32)
        .astype(jnp.bfloat16)
        .reshape(arrived.shape)
    )
    returned = lax.all_to_all(expert_out, "blk", split_axis=0, concat_axis=0, tiled=True)
    gathered_rows = returned.reshape(-1, normed.shape[1])[expert_slots].reshape(
        tok_count, TOPE, normed.shape[1]
    )
    mixing = gate_scores / jnp.sum(gate_scores, axis=1, keepdims=True)
    mixture = jnp.einsum("tk,tkd->td", mixing, gathered_rows, preferred_element_type=jnp.float32)
    return (hidden_state + mixture).astype(jnp.bfloat16)


LANES = 128
LOW_PART = 64
MESH = pl.DeviceIdType.MESH
LOWEST = -1e30
LOG2_E = 1.4426950408889634


def place_of(index):
    return lax.div(index, 4), lax.rem(lax.div(index, 2), 2), lax.rem(index, 2)


def index_of(z, x, c):
    return (z * 2 + x) * 2 + c


def nth_plane(k, z, planes):
    low = jnp.minimum(z, planes - 1 - z)
    near = k <= 2 * low
    far = jnp.where(near, lax.div(k + 1, 2), k - low)
    up = jnp.where(near, lax.rem(k, 2), (z < planes - 1 - z).astype(jnp.int32))
    return z + far * (2 * up - 1)


class Gather:
    def __init__(self, planes, parts, send_sem, recv_sem):
        self.planes, self.parts, self.send_sem, self.recv_sem = planes, parts, send_sem, recv_sem
        self.me = lax.axis_index("blk")
        self.z, self.x, self.c = place_of(self.me)

    def copy(self, part, way, block):
        z, x, c = self.z, self.x, self.c
        target = (
            index_of(z + 1, x, c),
            index_of(z - 1, x, c),
            index_of(z, 1 - x, c),
            index_of(z, x, 1 - c),
        )[way]
        buf, first, rows, _ = self.parts[part]
        piece = buf.at[block, first : first + rows]
        return pltpu.make_async_remote_copy(
            src_ref=piece,
            dst_ref=piece,
            send_sem=self.send_sem.at[part, way, block],
            recv_sem=self.recv_sem.at[part, block],
            device_id={"blk": target},
            device_id_type=MESH,
        )

    def across_first(self, part):
        return self.parts[part][3]

    def arrive(self, part, block):
        self.copy(part, 3, block).wait_recv()

    def along_z(self, part, plane, block, act):
        up = jnp.logical_and(plane <= self.z, self.z < self.planes - 1)
        down = jnp.logical_and(plane >= self.z, self.z > 0)

        @pl.when(up)
        def _():
            act(self.copy(part, 0, block))

        @pl.when(down)
        def _():
            act(self.copy(part, 1, block))

    def start(self):
        for part in range(len(self.parts)):
            for way in (2, 3):
                self.copy(part, way, self.me).start()
            self.along_z(part, self.z, self.me, lambda copy: copy.start())

    def take_first_across(self):
        block = index_of(self.z, 1 - self.x, self.c)
        for part in range(len(self.parts)):
            if self.across_first(part):
                self.arrive(part, block)
                self.along_z(part, self.z, block, lambda copy: copy.start())
                self.copy(part, 3, block).start()

    def take_column(self, k):
        plane = nth_plane(k, self.z, self.planes)
        block = index_of(plane, self.x, self.c)
        across = index_of(plane, 1 - self.x, self.c)
        for part in range(len(self.parts)):
            self.arrive(part, block)
            self.along_z(part, plane, block, lambda copy: copy.start())
            if not self.across_first(part):
                self.copy(part, 2, block).start()
            self.copy(part, 3, block).start()
        for part in range(len(self.parts)):
            if self.across_first(part):
                self.arrive(part, across)
                self.along_z(part, plane, across, lambda copy: copy.start())
                self.copy(part, 3, across).start()

    def take_across(self, k):
        plane = nth_plane(k, self.z, self.planes)
        block = index_of(plane, 1 - self.x, self.c)
        for part in range(len(self.parts)):
            if not self.across_first(part):
                self.arrive(part, block)
                self.copy(part, 3, block).start()

    def take_partner(self, k, x):
        plane = nth_plane(k, self.z, self.planes)
        for part in range(len(self.parts)):
            self.arrive(part, index_of(plane, x, 1 - self.c))

    def finish(self):
        @pl.loop(0, self.planes)
        def _(plane):
            block = index_of(plane, self.x, self.c)
            across = index_of(plane, 1 - self.x, self.c)
            for part in range(len(self.parts)):
                self.along_z(part, plane, block, lambda copy: copy.wait_send())
                self.copy(part, 3, block).wait_send()
                self.copy(part, 3, across).wait_send()
                if self.across_first(part):
                    self.along_z(part, plane, across, lambda copy: copy.wait_send())
                else:
                    self.copy(part, 2, block).wait_send()
            for part in range(len(self.parts)):
                if self.across_first(part):

                    @pl.when(plane == self.z)
                    def _():
                        self.copy(part, 2, block).wait_send()


def greet(planes, z, x, c):
    barrier = pltpu.get_barrier_semaphore()
    for target in (index_of(z, 1 - x, c), index_of(z, x, 1 - c)):
        pl.semaphore_signal(barrier, inc=1, device_id={"blk": target}, device_id_type=MESH)

    @pl.loop(0, planes)
    def _(plane):
        @pl.when(plane != z)
        def _():
            pl.semaphore_signal(
                barrier, inc=1, device_id={"blk": index_of(plane, x, c)}, device_id_type=MESH
            )

    pl.semaphore_wait(barrier, planes + 1)


def columns_of(rows, tokens):
    down = lax.broadcasted_iota(jnp.int32, (tokens, tokens), 0)
    right = lax.broadcasted_iota(jnp.int32, (tokens, tokens), 1)
    return [
        jnp.sum(jnp.where(down == right, rows[i : i + 1, :], 0.0), axis=1, keepdims=True)
        for i in range(rows.shape[0])
    ]


def layer_kernel(
    planes,
    cut_rows,
    q_any,
    k_any,
    v_any,
    new_k_any,
    new_v_any,
    ids_any,
    residual_any,
    weight_any,
    gain_any,
    experts_any,
    gates_any,
    gate_any,
    up_any,
    down_any,
    out_ref,
    kv_buf,
    q_rows,
    new_k_ref,
    new_v_ref,
    ids_in,
    residual_ref,
    weight_buf,
    gain_ref,
    experts_in,
    gates_in,
    gate_buf,
    up_buf,
    down_buf,
    q_buf,
    att_buf,
    max_buf,
    sum_buf,
    acc_buf,
    hidden_ref,
    row_buf,
    part_buf,
    core_out,
    core_in,
    across_out,
    across_in,
    plane_out,
    plane_in,
    o_out,
    o_in,
    stat_out,
    stat_in,
    local_sem,
    kv_send,
    kv_recv,
    give_send,
    give_recv,
    send_sem,
    recv_sem,
    row_send_sem,
    row_recv_sem,
    back_send,
    back_recv,
):
    keys = k_any.shape[0]
    tokens = residual_ref.shape[0]
    gather = Gather(planes, ((q_rows, 0, tokens, False),), send_sem, recv_sem)
    tokens, width = residual_ref.shape
    row_parts = ((row_buf, cut_rows, tokens - cut_rows, False),)
    if cut_rows:
        row_parts = ((row_buf, 0, cut_rows, True),) + row_parts
    row_gather = Gather(planes, row_parts, row_send_sem, row_recv_sem)
    me, z, x, c = gather.me, gather.z, gather.x, gather.c
    moves = (
        (k_any, kv_buf.at[0, 0:keys]),
        (v_any, kv_buf.at[0, keys : 2 * keys]),
        (q_any, q_rows.at[me, :, 0 : q_any.shape[1]]),
        (ids_any, ids_in),
        (new_k_any, new_k_ref),
        (new_v_any, new_v_ref),
        (experts_any, experts_in),
        (gates_any, gates_in),
        (residual_any, residual_ref),
        (gain_any, gain_ref),
        (weight_any, weight_buf),
        (gate_any.at[0], gate_buf),
        (up_any.at[0], up_buf),
        (down_any.at[0], down_buf),
    )
    loads = [
        pltpu.make_async_copy(source, target, local_sem.at[i])
        for i, (source, target) in enumerate(moves)
    ]
    for load in loads[:10]:
        load.start()
    greet(planes, z, x, c)
    def send_cache(to, source, target):
        return pltpu.make_async_remote_copy(
            src_ref=kv_buf.at[source],
            dst_ref=kv_buf.at[target],
            send_sem=kv_send.at[target],
            recv_sem=kv_recv.at[target],
            device_id={"blk": to},
            device_id_type=MESH,
        )

    to_core_own = send_cache(index_of(z, x, 1 - c), 0, 1)
    to_across_own = send_cache(index_of(z, 1 - x, c), 0, 2)
    to_core_across = send_cache(index_of(z, x, 1 - c), 2, 3)
    for load in loads[:4]:
        load.wait()
    to_across_own.start()
    to_core_own.start()
    lane = lax.broadcasted_iota(jnp.int32, (tokens, LANES), 1)
    ids = jnp.full((tokens, LANES), -1.0, jnp.float32)
    for choice, column in enumerate(columns_of(ids_in[...].astype(jnp.float32), tokens)):
        ids = jnp.where(lane == choice, column, ids)
    features = q_any.shape[1]
    q_rows[me, :, features:] = ids.astype(jnp.bfloat16)
    gather.along_z(0, z, me, lambda copy: copy.start())
    for load in loads[10:]:
        load.start()
    for load in loads[4:10]:
        load.wait()

    chunks, chunk_rows, _ = q_buf.shape
    heads = chunk_rows // tokens
    chunks_per_group = chunks // KEY_VALUE_HEADS
    factor = HEAD_SIZE ** (-0.5) * LOG2_E

    max_buf[...] = jnp.full(max_buf.shape, LOWEST, jnp.float32)
    sum_buf[...] = jnp.zeros(sum_buf.shape, jnp.float32)
    acc_buf[...] = jnp.zeros(acc_buf.shape, jnp.float32)

    def stack_heads(source):
        for chunk in range(chunks):
            for head in range(heads):
                at = (chunk * heads + head) * HEAD_SIZE
                q_buf[chunk, head * tokens : (head + 1) * tokens, :] = q_rows[
                    source, :, at : at + HEAD_SIZE
                ]

    stack_heads(me)
    for chunk in range(chunks):
        group = chunk // chunks_per_group
        lanes = slice(group * HEAD_SIZE, (group + 1) * HEAD_SIZE)
        scores = lax.dot_general(
            q_buf[chunk],
            new_k_ref[:, lanes],
            (((1,), (1,)), ((), ())),
            preferred_element_type=jnp.float32,
        )
        row = lax.rem(lax.broadcasted_iota(jnp.int32, scores.shape, 0), tokens)
        key = lax.broadcasted_iota(jnp.int32, scores.shape, 1)
        scores = jnp.where(key <= row, scores, -jnp.inf)
        top = jnp.max(scores, axis=1, keepdims=True)
        weights = jnp.exp2((scores - top) * factor)
        max_buf[z, chunk] = top
        sum_buf[z, chunk] = jnp.sum(weights, axis=1, keepdims=True)
        acc_buf[z, chunk] = jnp.dot(
            weights.astype(jnp.bfloat16), new_v_ref[:, lanes], preferred_element_type=jnp.float32
        )
    def give_back(plane, what):
        source, target = ((o_out, o_in), (stat_out, stat_in))[what]
        return lambda sender: pltpu.make_async_remote_copy(
            src_ref=source.at[plane],
            dst_ref=target.at[sender],
            send_sem=give_send.at[what, plane],
            recv_sem=give_recv.at[what, sender],
            device_id={"blk": index_of(plane, x, c)},
            device_id_type=MESH,
        )

    def take_queries(k):
        plane = nth_plane(k, z, planes)
        block = index_of(plane, x, c)
        gather.arrive(0, block)
        gather.along_z(0, plane, block, lambda copy: copy.start())

    last = planes - 1

    @pl.loop(0, 4 * planes)
    def _(step):
        pair, other_core = lax.div(step, 2), lax.rem(step, 2)
        middle = pair < 2 * planes - 3
        first_half = jnp.logical_or(pair < last, pair == 2 * planes - 3)
        k = jnp.where(
            pair < last,
            pair,
            jnp.where(middle, pair - (planes - 2), jnp.where(pair < 2 * planes - 1, last, 0)),
        )
        far = jnp.where(first_half, 0, 1)
        if True:
            plane = nth_plane(k, z, planes)
            owner = index_of(plane, x, c)

            @pl.when(other_core == 0)
            def _():
                @pl.when(jnp.logical_and(pair > 0, pair < last))
                def _():
                    take_queries(pair)

                @pl.when(pair == last)
                def _():
                    to_across_own.wait_recv()
                    to_core_across.start()

                @pl.when(pair == 2 * planes - 4)
                def _():
                    take_queries(last)

                stack_heads(owner)

            @pl.when(step == 1)
            def _():
                to_core_own.wait_recv()

            @pl.when(step == 2 * last + 1)
            def _():
                to_core_across.wait_recv()

            slot = 2 * far + other_core
            block = index_of(
                z,
                x + far * (1 - 2 * x),
                c + other_core * (1 - 2 * c),
            )
            chosen = q_rows[owner, :, features:].astype(jnp.float32)
            named = jnp.sum(
                jnp.where(chosen == block.astype(jnp.float32), 1.0, 0.0),
                axis=1,
                keepdims=True,
            )
            named = jnp.concatenate([named] * heads, axis=0) > 0.5
            for chunk in range(chunks):
                group = chunk // chunks_per_group
                lanes = slice(group * HEAD_SIZE, (group + 1) * HEAD_SIZE)
                scores = lax.dot_general(
                    q_buf[chunk],
                    kv_buf[slot, 0:keys, lanes],
                    (((1,), (1,)), ((), ())),
                    preferred_element_type=jnp.float32,
                )
                before = max_buf[plane, chunk]
                top = jnp.maximum(before, jnp.max(scores, axis=1, keepdims=True))
                weights = jnp.exp2((scores - top) * factor)
                scale = jnp.where(named, jnp.exp2((before - top) * factor), 1.0)
                total = jnp.sum(weights, axis=1, keepdims=True)
                mixed = jnp.dot(
                    weights.astype(jnp.bfloat16),
                    kv_buf[slot, keys : 2 * keys, lanes],
                    preferred_element_type=jnp.float32,
                )
                max_buf[plane, chunk] = jnp.where(named, top, before)
                sum_buf[plane, chunk] = sum_buf[plane, chunk] * scale + jnp.where(named, total, 0.0)
                acc_buf[plane, chunk] = acc_buf[plane, chunk] * scale + jnp.where(named, mixed, 0.0)

            @pl.when(jnp.logical_and(slot == 3, k > 0))
            def _():
                stat = jnp.zeros((tokens, LANES), jnp.float32)
                for chunk in range(chunks):
                    for head in range(heads):
                        number = chunk * heads + head
                        part = slice(head * tokens, (head + 1) * tokens)
                        stat = jnp.where(lane == number, max_buf[plane, chunk, part], stat)
                        stat = jnp.where(
                            lane == LOW_PART + number, sum_buf[plane, chunk, part], stat
                        )
                        o_out[plane, :, number * HEAD_SIZE : (number + 1) * HEAD_SIZE] = acc_buf[
                            plane, chunk, part
                        ].astype(jnp.bfloat16)
                stat_out[plane] = stat
                give_back(plane, 0)(z).start()
                give_back(plane, 1)(z).start()

            @pl.when(step == 0)
            def _():
                gates = gates_in[...]
                mixing = gates / jnp.sum(gates, axis=0, keepdims=True)
                spread = jnp.zeros((tokens, LANES), jnp.float32)
                columns = zip(
                    columns_of(experts_in[...].astype(jnp.float32), tokens),
                    columns_of(mixing, tokens),
                )
                for expert, share in columns:
                    expert = expert.astype(jnp.int32)
                    hit = jnp.logical_or(lane == expert, lane == expert + LOW_PART)
                    spread += jnp.where(hit, share, 0.0)
                rounded = spread.astype(jnp.bfloat16).astype(jnp.float32)
                row_buf[me, :, width:] = jnp.where(
                    lane < LOW_PART, rounded, spread - rounded
                ).astype(jnp.bfloat16)

    stat = jnp.zeros((tokens, LANES), jnp.float32)
    for number in range(chunks * heads):
        chunk, head = number // heads, number % heads
        part = slice(head * tokens, (head + 1) * tokens)
        stat = jnp.where(lane == number, max_buf[z, chunk, part], stat)
    stat_out[z] = stat
    for k in range(1, planes):
        plane = nth_plane(jnp.int32(k), z, planes)
        give_back(z, 0)(plane).wait_recv()
        give_back(z, 1)(plane).wait_recv()
        stat_out[z] = jnp.maximum(stat_out[z], stat_in[plane])
    tops = stat_out[z]
    for number in range(chunks * heads):
        chunk, head = number // heads, number % heads
        part = slice(head * tokens, (head + 1) * tokens)
        at = slice(number * HEAD_SIZE, (number + 1) * HEAD_SIZE)
        top = tops[:, number : number + 1]
        scale = jnp.exp2((max_buf[z, chunk, part] - top) * factor)
        total = sum_buf[z, chunk, part] * scale
        mixed = acc_buf[z, chunk, part] * scale
        for k in range(1, planes):
            plane = nth_plane(jnp.int32(k), z, planes)
            theirs = stat_in[plane]
            scale = jnp.exp2((theirs[:, number : number + 1] - top) * factor)
            total += theirs[:, LOW_PART + number : LOW_PART + number + 1] * scale
            mixed += o_in[plane, :, at].astype(jnp.float32) * scale
        att_buf[:, at] = (mixed / total).astype(jnp.bfloat16)
    for load in loads[10:]:
        load.wait()
    hidden = residual_ref[...].astype(jnp.float32) + jnp.dot(
        att_buf[...], weight_buf[...], preferred_element_type=jnp.float32
    )
    normed = (
        hidden
        * lax.rsqrt(jnp.mean(hidden * hidden, axis=-1, keepdims=True) + NORM_EPSILON)
        * gain_ref[...]
    )
    row_buf[me, :, :width] = normed.astype(jnp.bfloat16)
    row_gather.start()
    halves = core_out.shape[1]
    half_width = width // halves

    def cols(half):
        return slice(half * half_width, (half + 1) * half_width)

    def to_core(plane, half):
        return pltpu.make_async_remote_copy(
            src_ref=core_out.at[plane, half],
            dst_ref=core_in.at[plane, half],
            send_sem=back_send.at[0, plane, half],
            recv_sem=back_recv.at[0, plane, half],
            device_id={"blk": index_of(z, x, 1 - c)},
            device_id_type=MESH,
        )

    def to_across(plane, half):
        return pltpu.make_async_remote_copy(
            src_ref=across_out.at[plane, half],
            dst_ref=across_in.at[plane, half],
            send_sem=back_send.at[1, plane, half],
            recv_sem=back_recv.at[1, plane, half],
            device_id={"blk": index_of(z, 1 - x, c)},
            device_id_type=MESH,
        )

    def to_plane(plane, half, sender):
        return pltpu.make_async_remote_copy(
            src_ref=plane_out.at[plane, half],
            dst_ref=plane_in.at[sender, half],
            send_sem=back_send.at[2, plane, half],
            recv_sem=back_recv.at[2, sender, half],
            device_id={"blk": index_of(plane, x, c)},
            device_id_type=MESH,
        )

    hidden_ref[...] = hidden
    row_gather.take_first_across()

    @pl.loop(1, planes + 3)
    def _(k):
        @pl.when(k < planes)
        def _():
            row_gather.take_column(k)

        @pl.when(k <= planes)
        def _():
            place = k - 1
            plane = nth_plane(place, z, planes)
            row_gather.take_across(place)
            row_gather.take_partner(place, x)
            row_gather.take_partner(place, 1 - x)
            rows = row_buf[pl.ds(plane * 4, 4)].reshape(4 * tokens, width + LANES)
            shares = rows[:, width:].astype(jnp.float32)
            place_lane = lax.broadcasted_iota(jnp.int32, shares.shape, 1)
            hit = jnp.logical_or(place_lane == me, place_lane == me + LOW_PART)
            share = jnp.sum(jnp.where(hit, shares, 0.0), axis=1, keepdims=True)
            rows = rows[:, :width]
            gate_part = jnp.dot(rows, gate_buf[...], preferred_element_type=jnp.float32)
            up_part = jnp.dot(rows, up_buf[...], preferred_element_type=jnp.float32)
            inner = (gate_part / (1.0 + jnp.exp(-gate_part)) * up_part).astype(jnp.bfloat16)
            for half in range(halves):
                result = share * jnp.dot(
                    inner, down_buf[:, cols(half)], preferred_element_type=jnp.float32
                )
                part_buf[pl.ds(plane * 4, 4), :, cols(half)] = result.reshape(
                    4, tokens, half_width
                )
                for there in range(2):
                    core_out[plane, half, there] = part_buf[
                        index_of(plane, there, 1 - c), :, cols(half)
                    ].astype(jnp.bfloat16)
                to_core(plane, half).start()

        @pl.when(jnp.logical_and(k >= 2, k <= planes + 1))
        def _():
            plane = nth_plane(k - 2, z, planes)
            for half in range(halves):
                to_core(plane, half).wait_recv()
                across_out[plane, half] = (
                    part_buf[index_of(plane, 1 - x, c), :, cols(half)]
                    + core_in[plane, half, 1 - x].astype(jnp.float32)
                ).astype(jnp.bfloat16)
                to_across(plane, half).start()

        @pl.when(k >= 3)
        def _():
            plane = nth_plane(k - 3, z, planes)
            for half in range(halves):
                to_across(plane, half).wait_recv()
                total = (
                    part_buf[index_of(plane, x, c), :, cols(half)]
                    + core_in[plane, half, x].astype(jnp.float32)
                    + across_in[plane, half].astype(jnp.float32)
                )
                part_buf[index_of(plane, x, c), :, cols(half)] = total

                @pl.when(plane != z)
                def _():
                    plane_out[plane, half] = total.astype(jnp.bfloat16)
                    to_plane(plane, half, z).start()

    part_buf[me] += hidden_ref[...]

    @pl.loop(0, planes)
    def _(plane):
        @pl.when(plane != z)
        def _():
            for half in range(halves):
                to_plane(z, half, plane).wait_recv()
                part_buf[me, :, cols(half)] += plane_in[plane, half].astype(jnp.float32)

    out_ref[...] = part_buf[me].astype(jnp.bfloat16)

    @pl.loop(0, planes)
    def _(plane):
        for half in range(halves):
            to_core(plane, half).wait_send()
            to_across(plane, half).wait_send()

            @pl.when(plane != z)
            def _():
                to_plane(plane, half, z).wait_send()

    @pl.loop(0, planes)
    def _(plane):
        gather.along_z(0, plane, index_of(plane, x, c), lambda copy: copy.wait_send())

        @pl.when(plane != z)
        def _():
            give_back(plane, 0)(z).wait_send()
            give_back(plane, 1)(z).wait_send()

    for copy in (to_core_own, to_across_own, to_core_across):
        copy.wait_send()
    row_gather.finish()


def gathered(*operands):
    (
        queries,
        cache_keys,
        cache_values,
        new_keys,
        new_values,
        block_ids,
        residual,
        out_weight,
        norm_gain,
        expert_ids,
        gate_scores,
        w_gate,
        w_up,
        w_down,
    ) = operands
    parties = lax.axis_size("blk")
    planes = parties // 4
    tokens, width = residual.shape
    keys, lanes = cache_keys.shape
    bf16, f32 = jnp.bfloat16, jnp.float32
    chunks, halves = 4, 2
    chunk_rows = tokens * QUERY_HEADS // chunks
    cut_rows = tokens // 4 // 16 * 16
    outside = pl.BlockSpec(memory_space=pltpu.HBM)
    inputs = (
        queries,
        cache_keys,
        cache_values,
        new_keys,
        new_values,
        block_ids.T,
        residual,
        out_weight,
        norm_gain[None, :],
        expert_ids.T,
        gate_scores.T,
        w_gate,
        w_up,
        w_down,
    )

    def like(array):
        return pltpu.VMEM(array.shape, array.dtype)

    back = (planes, halves, tokens, width // halves)
    core_back = (planes, halves, 2, tokens, width // halves)
    row_parts = 2 if cut_rows else 1
    return pl.pallas_call(
        functools.partial(layer_kernel, planes, cut_rows),
        out_shape=jax.ShapeDtypeStruct((tokens, width), bf16),
        in_specs=[outside] * len(inputs),
        out_specs=pl.BlockSpec(memory_space=pltpu.VMEM),
        scratch_shapes=[
            pltpu.VMEM((4, 2 * keys, lanes), bf16),
            pltpu.VMEM((parties, tokens, queries.shape[1] + LANES), bf16),
            like(inputs[3]),
            like(inputs[4]),
            like(inputs[5]),
            like(inputs[6]),
            like(inputs[7]),
            like(inputs[8]),
            like(inputs[9]),
            like(inputs[10]),
            pltpu.VMEM(w_gate.shape[1:], bf16),
            pltpu.VMEM(w_up.shape[1:], bf16),
            pltpu.VMEM(w_down.shape[1:], bf16),
            pltpu.VMEM((chunks, chunk_rows, HEAD_SIZE), bf16),
            pltpu.VMEM((tokens, QUERY_HEADS * HEAD_SIZE), bf16),
            pltpu.VMEM((planes, chunks, chunk_rows, 1), f32),
            pltpu.VMEM((planes, chunks, chunk_rows, 1), f32),
            pltpu.VMEM((planes, chunks, chunk_rows, HEAD_SIZE), f32),
            pltpu.VMEM((tokens, width), f32),
            pltpu.VMEM((parties, tokens, width + LANES), bf16),
            pltpu.VMEM((parties, tokens, width), f32),
            pltpu.VMEM(core_back, bf16),
            pltpu.VMEM(core_back, bf16),
            pltpu.VMEM(back, bf16),
            pltpu.VMEM(back, bf16),
            pltpu.VMEM(back, bf16),
            pltpu.VMEM(back, bf16),
            pltpu.VMEM((planes,) + queries.shape, bf16),
            pltpu.VMEM((planes,) + queries.shape, bf16),
            pltpu.VMEM((planes, tokens, LANES), f32),
            pltpu.VMEM((planes, tokens, LANES), f32),
            pltpu.SemaphoreType.DMA((14,)),
            pltpu.SemaphoreType.DMA((4,)),
            pltpu.SemaphoreType.DMA((4,)),
            pltpu.SemaphoreType.DMA((2, planes)),
            pltpu.SemaphoreType.DMA((2, planes)),
            pltpu.SemaphoreType.DMA((1, 4, parties)),
            pltpu.SemaphoreType.DMA((1, parties)),
            pltpu.SemaphoreType.DMA((row_parts, 4, parties)),
            pltpu.SemaphoreType.DMA((row_parts, parties)),
            pltpu.SemaphoreType.DMA((3, planes, halves)),
            pltpu.SemaphoreType.DMA((3, planes, halves)),
        ],
        compiler_params=pltpu.CompilerParams(
            collective_id=0, has_side_effects=True, vmem_limit_bytes=60 << 20
        ),
        name="layer",
    )(*inputs)


GATHER_LIMIT_BYTES = 24 << 20


def layer(*operands):
    parties = lax.axis_size("blk")
    keys, values = operands[1], operands[2]
    cache_bytes = parties * (keys.size + values.size) * keys.dtype.itemsize
    fits = cache_bytes <= GATHER_LIMIT_BYTES and parties % 4 == 0 and parties >= 12 and parties <= LOW_PART
    return gathered(*operands) if fits else body(*operands)


def solution(mesh):
    placed = (
        P(("groups", "blk"), None),
        P(("groups", "blk"), None),
        P(("groups", "blk"), None),
        P(("groups", "blk"), None),
        P(("groups", "blk"), None),
        P(("groups", "blk"), None),
        P(("groups", "blk"), None),
        P(),
        P(),
        P(("groups", "blk"), None),
        P(("groups", "blk"), None),
        P("blk", None, None),
        P("blk", None, None),
        P("blk", None, None),
    )
    return jax.shard_map(
        layer, mesh=mesh, in_specs=placed, out_specs=P(("groups", "blk"), None), check_vma=False
    )
```
